256 devices in a mesh: tensor: 8 (over x, core), req: 32 (over y, z).
Axes of the slice: x: 4, y: 4, z: 8, core: 2. Of those that a mesh axis runs over, the one named last changes fastest.
Arguments:
- attention_output: bfloat16 [16384, 4096], P('req', 'tensor'), may hold values from -6 to 6
- residual: bfloat16 [16384, 8192], P('req', 'tensor'), may hold values from -6 to 6
- projection_weight: bfloat16 [4096, 8192], P('tensor'), may hold values from -0.09375 to 0.09375
- adapter_down_maps: bfloat16 [256, 4096, 64], P('req', 'tensor'), may hold values from -0.09375 to 0.09375
- adapter_up_maps: bfloat16 [256, 64, 8192], P('req', None, 'tensor'), may hold values from -0.75 to 0.75
- adapter_pool_slot: int32 [256], replicated, may hold values from 0 to 255, as said below
- request_adapter_id: int32 [32, 32], replicated, may hold values from 0 to 255, as said below
- request_token_length: int32 [32, 32], P('req'), may hold values from 1 to 32, 512 in all within a row
Outputs:
- mixed: bfloat16 [16384, 8192], P('req', 'tensor')
The draws below stay inside these ranges and needn't reach their ends.
Inputs may be any that keep to these rules, and one draw needn't show every extreme that they name: `adapter_pool_slot`: each slot appears once; the slot s lies on index s // 8 of req, its owner. `request_adapter_id`: the 32 requests of one group use adapters with 32 distinct owners. `request_token_length`: each group's lengths sum to 512; in each group the largest is exactly 32.
All inputs are finite; a program needn't handle non-finite values.
Results may differ from the reference program's by a relative error of at most 0.014.
Values may be sent and summed in bfloat16 or wider, within the bound.
No kernel may reach another device: no remote copies, remote signals or barrier semaphores. Data moves between devices by JAX's collectives and lax.ppermute only.
A program may use at most 128 MiB of HBM per device.

```python
import math
import jax
import jax.numpy as jnp
import numpy as np
from jax import lax

MODEL_WIDTH = 8192
ADAPTER_RANK = 64
TOK_DEV = 512
ADAPT_DEV = 8
ATTENTION_WIDTH = 4096
GROUPS = 32
REQ_GRP = 32
MOST = 32
ADAPTER_POOL = 256
TOKENS = 16384
N_TENSOR = 8


def pick_adapters(key):
    base_key = jax.random.fold_in(key, 7)
    slot_key, heat_key, pick_key, row_key = jax.random.split(base_key, 4)
    request_slots = jax.random.permutation(slot_key, ADAPTER_POOL).astype(jnp.int32)
    heat = jax.random.randint(heat_key, (GROUPS,), 0, 3 * GROUPS)
    noise = jax.random.randint(pick_key, (GROUPS, GROUPS), 0, 2 * GROUPS)
    scores = (heat[None, :] + noise) * GROUPS + jnp.arange(GROUPS, dtype=jnp.int32)[None, :]
    owners = lax.top_k(scores.astype(jnp.int32), REQ_GRP)[1].astype(jnp.int32)
    local = jax.random.randint(row_key, (GROUPS, REQ_GRP), 0, ADAPT_DEV).astype(jnp.int32)
    wanted = owners * ADAPT_DEV + local
    inverse = jnp.argsort(request_slots).astype(jnp.int32)
    return (request_slots, jnp.take(inverse, wanted).astype(jnp.int32))


def draw_adapter_pool_slot(key, part):
    return pick_adapters(key)[0]


def draw_request_adapter_id(key, part):
    return pick_adapters(key)[1]


def block_scale(stream_key, extent, shards, smallest, top_value):
    loudness = 1.0
    for axis_at, parts in shards:
        steps = jax.random.uniform(jax.random.fold_in(jax.random.fold_in(stream_key, 6), axis_at), (parts,), jnp.float32, smallest / len(shards), top_value / len(shards))
        loudness = loudness * jnp.repeat(jnp.exp(steps), extent[axis_at] // parts).reshape((-1,) + (1,) * (len(extent) - 1 - axis_at))
    return loudness


def split_up(count, total, reach, slope):
    weights = [(1 << 20) // math.isqrt(grade ** slope) + 1 for grade in range(2, count + 1)]
    surplus, counts = total - reach - (count - 1), [1] * (count - 1)
    while surplus > 0:
        free = [i for i in range(count - 1) if counts[i] < reach]
        whole, budget = sum([weights[i] for i in free]), surplus
        for i in free:
            extra = min(reach - counts[i], max(1, budget * weights[i] // whole), surplus)
            counts[i] = counts[i] + extra
            surplus = surplus - extra
    return np.array([reach] + counts)


def ragged(stream_key, amount, total, most, skew):
    if amount == 2:
        one = jax.random.randint(stream_key, (), max(1, total - most), min(most, total - 1) + 1)
        return jnp.stack([one, total - one])
    sizes = jnp.asarray(split_up(amount, total, most, skew), jnp.int32)
    pairs = (amount - 1) // 2
    donor, receiver = sizes[1:1 + 2 * pairs:2], sizes[2:2 + 2 * pairs:2]
    margin = jnp.minimum(donor - 1, most - receiver)
    passed = jax.random.randint(jax.random.fold_in(stream_key, 1), (pairs,), 0, 1 << 20) % (margin + 1)
    sizes = sizes.at[1:1 + 2 * pairs:2].set(donor - passed).at[2:2 + 2 * pairs:2].set(receiver + passed)
    return sizes[jax.random.permutation(jax.random.fold_in(stream_key, 2), amount)]


def bell_draw(stream_key, shape, scale, limit, pieces=(), held_as=jnp.bfloat16):
    array = jax.random.normal(stream_key, shape, jnp.float32) * scale
    if len(pieces) > 0:
        array = block_scale(stream_key, shape, pieces, -0.22, 0.18) * array
    return jnp.clip(array, min=-limit, max=limit).astype(held_as)


def setup_inputs(seed: int = 0) -> dict:
    seeds = jax.random.split(jax.random.key(seed), 9)
    return {
        "attention_output": bell_draw(seeds[0], (TOKENS, ATTENTION_WIDTH), 1.0, 6.0, ((0, 32), (1, 8))),
        "residual": bell_draw(seeds[1], (TOKENS, MODEL_WIDTH), 1.0, 6.0, ((0, 32), (1, 8))),
        "projection_weight": bell_draw(seeds[2], (ATTENTION_WIDTH, MODEL_WIDTH), ATTENTION_WIDTH ** -0.5, 0.09375, ((0, 8),)),
        "adapter_down_maps": bell_draw(seeds[3], (ADAPTER_POOL, ATTENTION_WIDTH, ADAPTER_RANK), ATTENTION_WIDTH ** -0.5, 0.09375, ((0, 32), (1, 8))),
        "adapter_up_maps": bell_draw(seeds[4], (ADAPTER_POOL, ADAPTER_RANK, MODEL_WIDTH), ADAPTER_RANK ** -0.5, 0.75, ((0, 32), (2, 8))),
        "adapter_pool_slot": draw_adapter_pool_slot(jax.random.fold_in(seeds[8], 71), 0),
        "request_adapter_id": draw_request_adapter_id(jax.random.fold_in(seeds[8], 71), 0),
        "request_token_length": jax.vmap(lambda own: ragged(own, REQ_GRP, TOK_DEV, MOST, 2))(jax.random.split(seeds[7], GROUPS)).reshape((GROUPS, REQ_GRP)).astype(jnp.int32),
    }


def reference(attention_output, residual, projection_weight, adapter_down_maps, adapter_up_maps, adapter_pool_slot, request_adapter_id, request_token_length):
    width = ATTENTION_WIDTH // N_TENSOR

    def one_group(group):
        rows = lax.dynamic_slice_in_dim(attention_output, group * TOK_DEV, TOK_DEV, 0)
        stream = lax.dynamic_slice_in_dim(residual, group * TOK_DEV, TOK_DEV, 0)
        base = jnp.zeros((TOK_DEV, MODEL_WIDTH), jnp.float32)
        for shard in range(N_TENSOR):
            part = jnp.dot(rows[:, shard * width:(shard + 1) * width], projection_weight[shard * width:(shard + 1) * width], preferred_element_type=jnp.float32)
            base = base + part.astype(jnp.bfloat16).astype(jnp.float32)
        request_slots = jnp.take(adapter_pool_slot, request_adapter_id[group])
        lengths = request_token_length[group]
        ends = jnp.cumsum(lengths)
        starts = (ends - lengths).astype(jnp.int32)
        padded = jnp.concatenate([rows, jnp.zeros((MOST, ATTENTION_WIDTH), rows.dtype)], 0)
        delta = jnp.zeros((TOK_DEV + MOST, MODEL_WIDTH), jnp.float32)
        inside = jnp.arange(MOST, dtype=jnp.int32)
        for request_number in range(REQ_GRP):
            start = starts[request_number].astype(jnp.int32)
            request_span = lax.dynamic_slice_in_dim(padded, start, MOST, 0)
            token_mask = (inside < lengths[request_number]).astype(jnp.float32)[:, None]
            reduced_rows = (token_mask * jnp.dot(request_span, adapter_down_maps[request_slots[request_number]], preferred_element_type=jnp.float32)).astype(jnp.bfloat16)
            raised_output = token_mask * jnp.dot(reduced_rows, adapter_up_maps[request_slots[request_number]], preferred_element_type=jnp.float32)
            current = lax.dynamic_slice_in_dim(delta, start, MOST, 0)
            delta = lax.dynamic_update_slice_in_dim(delta, current + raised_output, start, 0)
        return (stream.astype(jnp.float32) + base + delta[:TOK_DEV]).astype(jnp.bfloat16)

    blocks = lax.map(one_group, jnp.arange(GROUPS, dtype=jnp.int32))
    return blocks.reshape(TOKENS, MODEL_WIDTH)
```

```python
import functools

import jax
import jax.numpy as jnp
from jax import lax
from jax.experimental import pallas as pl
from jax.experimental.pallas import tpu as pltpu
from jax.sharding import PartitionSpec as P


BF = jnp.bfloat16
F32 = jnp.float32
VM = pl.BlockSpec(memory_space=pltpu.VMEM)
SM = pl.BlockSpec(memory_space=pltpu.SMEM)


def cost(flops, nbytes):
    return pl.CostEstimate(flops=int(flops), transcendentals=0, bytes_accessed=int(nbytes))


def pack_kernel(me_ref, len_ref, id_ref, slot_ref, x_ref, out_ref, sel_ref, *, pool, most):
    requests = len_ref.shape[1]
    tokens = x_ref.shape[0]
    rows = lax.broadcasted_iota(jnp.int32, (most, tokens), 0)
    ahead = lax.broadcasted_iota(jnp.int32, (most, tokens), 1) - rows
    me = me_ref[0]
    start = jnp.int32(0)
    for r in range(requests):
        owner = lax.div(slot_ref[id_ref[me, r]], jnp.int32(pool))
        count = len_ref[0, r]
        hit = (ahead == start) & (rows < count)
        at = pl.multiple_of(owner * most, most)
        sel_ref[pl.ds(at, most), :] = jnp.where(hit, 1.0, 0.0).astype(BF)
        start = start + count
    out_ref[...] = jnp.dot(sel_ref[...], x_ref[...], preferred_element_type=F32).astype(BF)


def unpack_matrix_kernel(me_ref, len_ref, id_ref, slot_ref, sel_ref, *, pool, most):
    requests = len_ref.shape[1]
    tokens = sel_ref.shape[0]
    lanes = 128
    per = lanes // most
    tok = lax.broadcasted_iota(jnp.int32, (tokens, lanes), 0)
    lane = lax.broadcasted_iota(jnp.int32, (tokens, lanes), 1)
    behind = tok - lane
    sel_ref[...] = jnp.zeros_like(sel_ref)
    me = me_ref[0]
    start = jnp.int32(0)
    for r in range(requests):
        owner = lax.div(slot_ref[id_ref[me, r]], jnp.int32(pool))
        count = len_ref[0, r]
        block = lax.div(owner, jnp.int32(per))
        off = (owner - block * per) * most
        hit = (behind == start - off) & (tok >= start) & (tok < start + count)
        at = pl.ds(pl.multiple_of(block * lanes, lanes), lanes)
        sel_ref[:, at] = sel_ref[:, at] + jnp.where(hit, 1.0, 0.0).astype(BF)
        start = start + count


def down_kernel(idx_ref, x_ref, d_ref, out_ref, *, pool):
    rank = out_ref.shape[0]
    every = lax.dot_general(d_ref[...], x_ref[...], (((1,), (1,)), ((), ())), preferred_element_type=F32)
    idx = idx_ref[...]
    acc = jnp.zeros(out_ref.shape, F32)
    for a in range(pool):
        acc = acc + jnp.where(idx == a, every[a * rank:(a + 1) * rank], 0.0)
    out_ref[...] = acc.astype(BF)


def up_kernel(idx_ref, l_ref, r_ref, u_ref, out_ref, *, pool):
    low = (l_ref[...].astype(F32) + r_ref[...].astype(F32)).astype(BF).astype(F32)
    idx = idx_ref[...]
    spread = jnp.concatenate([jnp.where(idx == a, low, 0.0).astype(BF) for a in range(pool)], 0)
    out_ref[...] = lax.dot_general(
        spread, u_ref[...], (((0,), (0,)), ((), ())), preferred_element_type=F32
    ).astype(BF)


def pair_dot_kernel(t_ref, x_ref, w_ref, out_ref):
    out_ref[0] = jnp.dot(x_ref[...], w_ref[...], preferred_element_type=F32).astype(BF)


def own_dot_kernel(t_ref, x_ref, w_ref, p_ref, ka_ref, sa_ref, kb_ref, sb_ref):
    half = x_ref.shape[0] // 2
    both = (jnp.dot(x_ref[...], w_ref[...], preferred_element_type=F32) + p_ref[0].astype(F32)).astype(BF)
    top, low = both[:half], both[half:]
    j = pl.program_id(0)

    @pl.when(j == 0)
    def _():
        ka_ref[0] = top
        kb_ref[0] = low

    @pl.when(j == 1)
    def _():
        sa_ref[0] = top
        kb_ref[1] = low

    @pl.when(j == 2)
    def _():
        ka_ref[1] = top
        sb_ref[0] = low

    @pl.when(j == 3)
    def _():
        sa_ref[1] = top
        sb_ref[1] = low


def final_kernel(sel_ref, ret_ref, res_ref, ka_ref, ra_ref, za_ref, kb_ref, rb_ref, zb_ref, out_ref):
    half = res_ref.shape[0] // 2
    delta = jnp.dot(sel_ref[...], ret_ref[...], preferred_element_type=F32)
    base_a = ka_ref[0].astype(F32) + ra_ref[0].astype(F32) + za_ref[...].astype(F32)
    base_b = kb_ref[0].astype(F32) + rb_ref[0].astype(F32) + zb_ref[...].astype(F32)
    out_ref[:half] = (res_ref[:half].astype(F32) + base_a + delta[:half]).astype(BF)
    out_ref[half:] = (res_ref[half:].astype(F32) + base_b + delta[half:]).astype(BF)


def one_block(x, residual, weight, down, up, pool_slot, req_id, req_len):
    groups = lax.axis_size("req")
    n_t = lax.axis_size("tensor")
    me = lax.axis_index("req").astype(jnp.int32)
    t = lax.axis_index("tensor").astype(jnp.int32)
    tokens, features = x.shape
    pool = down.shape[0]
    rank = down.shape[2]
    cols = residual.shape[1]
    requests = req_len.shape[1]
    most = 2 * tokens // requests
    slots = groups * most
    half = tokens // 2
    me1 = me.reshape(1)
    t1 = t.reshape(1)
    xor = lambda m: [(i, i ^ m) for i in range(n_t)]
    sds = jax.ShapeDtypeStruct

    outgoing = pl.pallas_call(
        functools.partial(pack_kernel, pool=pool, most=most),
        out_shape=sds((slots, features), BF),
        in_specs=[SM, SM, SM, SM, VM],
        out_specs=VM,
        scratch_shapes=[pltpu.VMEM((slots, tokens), BF)],
        cost_estimate=cost(2 * slots * tokens * features, 2 * (slots + tokens) * features),
        name="pack",
    )(me1, req_len, req_id, pool_slot, x)
    arrived = lax.all_to_all(outgoing.reshape(groups, most, features), "req", split_axis=0, concat_axis=0, tiled=True)

    x, _ = lax.optimization_barrier((x, outgoing))

    def blocks(j):
        return j ^ (j >> 1)

    k = n_t // 2
    wide = 2 * tokens * features * cols * k
    to_pair = pl.pallas_call(
        pair_dot_kernel,
        out_shape=sds((k, tokens, cols), BF),
        grid_spec=pltpu.PrefetchScalarGridSpec(
            num_scalar_prefetch=1,
            grid=(k,),
            in_specs=[
                pl.BlockSpec((tokens, features), lambda j, t_ref: (0, 0)),
                pl.BlockSpec((features, cols), lambda j, t_ref: (0, t_ref[0] ^ 1 ^ (2 * blocks(j)))),
            ],
            out_specs=pl.BlockSpec((1, tokens, cols), lambda j, t_ref: (j, 0, 0)),
        ),
        cost_estimate=cost(wide, 2 * k * cols * (tokens + features)),
        name="pair_dot",
    )(t1, x, weight)
    from_pair = lax.ppermute(to_pair, "tensor", xor(1))

    piece = sds((2, half, cols), BF)
    keep = pl.BlockSpec((2, half, cols), lambda j, t_ref: (0, 0, 0))
    ka, sa, kb, sb = pl.pallas_call(
        own_dot_kernel,
        out_shape=[piece] * 4,
        grid_spec=pltpu.PrefetchScalarGridSpec(
            num_scalar_prefetch=1,
            grid=(k,),
            in_specs=[
                pl.BlockSpec((tokens, features), lambda j, t_ref: (0, 0)),
                pl.BlockSpec((features, cols), lambda j, t_ref: (0, t_ref[0] ^ (2 * blocks(j)))),
                pl.BlockSpec((1, tokens, cols), lambda j, t_ref: (j, 0, 0)),
            ],
            out_specs=[keep] * 4,
        ),
        cost_estimate=cost(wide, 2 * k * cols * (2 * tokens + features)),
        name="own_dot",
    )(t1, x, weight, from_pair)

    ids = jnp.arange(pool_slot.shape[0], dtype=jnp.int32)
    held = me * pool + jnp.arange(pool, dtype=jnp.int32)
    id_of = jnp.sum(jnp.where(pool_slot[None, :] == held[:, None], ids[None, :], 0), 1)
    uses = req_id[:, :, None] == id_of[None, None, :]
    idx = jnp.sum(jnp.where(uses, jnp.arange(pool, dtype=jnp.int32), 0), (1, 2))
    idx = jnp.broadcast_to(idx[:, None], (groups, most)).reshape(1, slots)

    sel = pl.pallas_call(
        functools.partial(unpack_matrix_kernel, pool=pool, most=most),
        out_shape=sds((tokens, slots), BF),
        in_specs=[SM, SM, SM, SM],
        out_specs=VM,
        cost_estimate=cost(8 * slots * tokens, 2 * slots * tokens),
        name="unpack_matrix",
    )(me1, req_len, req_id, pool_slot)

    arrived, idx, sel, ka, sa, kb, sb = lax.optimization_barrier((arrived, idx, sel, ka, sa, kb, sb))
    low = pl.pallas_call(
        functools.partial(down_kernel, pool=pool),
        out_shape=sds((rank, slots), BF),
        in_specs=[VM, VM, VM],
        out_specs=VM,
        cost_estimate=cost(2 * slots * pool * rank * features, 2 * slots * features),
        name="down",
    )(idx, arrived.reshape(slots, features), jnp.swapaxes(down, 1, 2).reshape(pool * rank, features))
    for m in (1, 2):
        other = lax.ppermute(low, "tensor", xor(m))
        low = (low.astype(F32) + other.astype(F32)).astype(BF)
    other = lax.ppermute(low, "tensor", xor(6))

    step = slots // 4
    raised = pl.pallas_call(
        functools.partial(up_kernel, pool=pool),
        out_shape=sds((slots, cols), BF),
        grid=(4,),
        in_specs=[
            pl.BlockSpec((1, step), lambda i: (0, i)),
            pl.BlockSpec((rank, step), lambda i: (0, i)),
            pl.BlockSpec((rank, step), lambda i: (0, i)),
            pl.BlockSpec((pool * rank, cols), lambda i: (0, 0)),
        ],
        out_specs=pl.BlockSpec((step, cols), lambda i: (i, 0)),
        cost_estimate=cost(2 * slots * pool * rank * cols, 2 * slots * cols),
        name="up",
    )(idx, low, other, up.reshape(pool * rank, cols))
    raised, sa, sb = lax.optimization_barrier((raised, sa, sb))
    returned = lax.all_to_all(
        raised.reshape(groups, most, cols), "req", split_axis=0, concat_axis=0, tiled=True
    )

    ra = lax.ppermute(sa, "tensor", xor(2))
    rb = lax.ppermute(sb, "tensor", xor(6))
    za = lax.ppermute((ka[1].astype(F32) + ra[1].astype(F32)).astype(BF), "tensor", xor(6))
    zb = lax.ppermute((kb[1].astype(F32) + rb[1].astype(F32)).astype(BF), "tensor", xor(2))

    wide = cols // 4
    lead = pl.BlockSpec((1, half, wide), lambda i: (0, 0, i))
    flat = pl.BlockSpec((half, wide), lambda i: (0, i))
    return pl.pallas_call(
        final_kernel,
        out_shape=sds((tokens, cols), BF),
        grid=(4,),
        in_specs=[
            pl.BlockSpec((tokens, slots), lambda i: (0, 0)),
            pl.BlockSpec((slots, wide), lambda i: (0, i)),
            pl.BlockSpec((tokens, wide), lambda i: (0, i)),
            lead, lead, flat, lead, lead, flat,
        ],
        out_specs=pl.BlockSpec((tokens, wide), lambda i: (0, i)),
        cost_estimate=cost(2 * tokens * slots * cols, 2 * cols * (slots + 4 * tokens)),
        name="final",
    )(sel, returned.reshape(slots, cols), residual, ka, ra, za, kb, rb, zb)


def solution(mesh):
    in_specs = (
        P("req", "tensor"),
        P("req", "tensor"),
        P("tensor", None),
        P("req", "tensor", None),
        P("req", None, "tensor"),
        P(),
        P(),
        P("req", None),
    )
    return jax.shard_map(one_block, mesh=mesh, in_specs=in_specs, out_specs=P("req", "tensor"), check_vma=False)
```

```python
import functools

import jax
import jax.numpy as jnp
from jax import lax
from jax.experimental import pallas as pl
from jax.experimental.pallas import tpu as pltpu
from jax.sharding import PartitionSpec as P


BF = jnp.bfloat16
F32 = jnp.float32
VM = pl.BlockSpec(memory_space=pltpu.VMEM)
SM = pl.BlockSpec(memory_space=pltpu.SMEM)


SMALL = pltpu.CompilerParams(vmem_limit_bytes=24 * 2**20)


def cost(flops, nbytes):
    return pl.CostEstimate(flops=int(flops), transcendentals=0, bytes_accessed=int(nbytes))


def pack_kernel(me_ref, len_ref, id_ref, slot_ref, x_ref, out_ref, sel_ref, *, pool, most):
    requests = len_ref.shape[1]
    tokens = x_ref.shape[0]
    rows = lax.broadcasted_iota(jnp.int32, (most, tokens), 0)
    ahead = lax.broadcasted_iota(jnp.int32, (most, tokens), 1) - rows
    me = me_ref[0]
    start = jnp.int32(0)
    for r in range(requests):
        owner = lax.div(slot_ref[id_ref[me, r]], jnp.int32(pool))
        count = len_ref[0, r]
        hit = (ahead == start) & (rows < count)
        at = pl.multiple_of(owner * most, most)
        sel_ref[pl.ds(at, most), :] = jnp.where(hit, 1.0, 0.0).astype(BF)
        start = start + count
    out_ref[...] = jnp.dot(sel_ref[...], x_ref[...], preferred_element_type=F32).astype(BF)


def unpack_matrix_kernel(me_ref, len_ref, id_ref, slot_ref, sel_ref, *, pool, most):
    requests = len_ref.shape[1]
    tokens = sel_ref.shape[0]
    lanes = 128
    per = lanes // most
    tok = lax.broadcasted_iota(jnp.int32, (tokens, lanes), 0)
    lane = lax.broadcasted_iota(jnp.int32, (tokens, lanes), 1)
    behind = tok - lane
    sel_ref[...] = jnp.zeros_like(sel_ref)
    me = me_ref[0]
    start = jnp.int32(0)
    for r in range(requests):
        owner = lax.div(slot_ref[id_ref[me, r]], jnp.int32(pool))
        count = len_ref[0, r]
        block = lax.div(owner, jnp.int32(per))
        off = (owner - block * per) * most
        hit = (behind == start - off) & (tok >= start) & (tok < start + count)
        at = pl.ds(pl.multiple_of(block * lanes, lanes), lanes)
        sel_ref[:, at] = sel_ref[:, at] + jnp.where(hit, 1.0, 0.0).astype(BF)
        start = start + count


def down_kernel(code_ref, x_ref, d_ref, out_ref, *, pool):
    rank = out_ref.shape[1] // 2
    half = out_ref.shape[0]
    every = lax.dot_general(x_ref[...], d_ref[...], (((1,), (1,)), ((), ())), preferred_element_type=F32)
    code = code_ref[...]
    acc = jnp.zeros(code.shape, F32)
    for b in range(pool // 2):
        acc = acc + jnp.where(code == 2 * b, every[:, 2 * b * rank:2 * (b + 1) * rank], 0.0)
    acc = acc + pltpu.roll(acc, rank, 1)
    first = lax.broadcasted_iota(jnp.int32, out_ref.shape, 1) < rank
    out_ref[...] = jnp.where(first, acc[:half], acc[half:]).astype(BF)


def add_kernel(*refs):
    n = len(refs) // 3
    for i in range(n):
        refs[2 * n + i][...] = (refs[i][...].astype(F32) + refs[n + i][...].astype(F32)).astype(BF)


def add_split_kernel(l_ref, r_ref, a_ref, b_ref):
    both = (l_ref[...].astype(F32) + r_ref[...].astype(F32)).astype(BF)
    half = a_ref.shape[0]
    a_ref[...] = both[:half]
    b_ref[...] = both[half:]


def up_kernel(code_ref, a_ref, ra_ref, b_ref, rb_ref, u_ref, out_ref, *, pool):
    i = pl.program_id(0)
    rows, lanes = a_ref.shape
    rank = lanes // 2
    even = lax.rem(i, 2) == 0
    a = a_ref[...].astype(F32) + ra_ref[...].astype(F32)
    b = b_ref[...].astype(F32) + rb_ref[...].astype(F32)
    low = jnp.where(even, a, b).astype(BF).astype(F32)
    first = lax.broadcasted_iota(jnp.int32, low.shape, 1) < rank
    mine = jnp.logical_xor(first, i >= 2)
    low = jnp.where(mine, low, pltpu.roll(low, rank, 1))
    code = code_ref[pl.ds(pl.multiple_of(i * rows, rows), rows), :]
    spread = jnp.concatenate(
        [jnp.where(code == 2 * k, low, 0.0).astype(BF) for k in range(pool // 2)], 1
    )
    out_ref[...] = jnp.dot(spread, u_ref[...], preferred_element_type=F32).astype(BF)


def pair_dot_kernel(t_ref, x_ref, w_ref, out_ref):
    out_ref[0] = jnp.dot(x_ref[...], w_ref[...], preferred_element_type=F32).astype(BF)


def own_dot_kernel(t_ref, x_ref, w_ref, p_ref, ka_ref, sa_ref, kb_ref, sb_ref):
    half = x_ref.shape[0] // 2
    both = (jnp.dot(x_ref[...], w_ref[...], preferred_element_type=F32) + p_ref[0].astype(F32)).astype(BF)
    top, low = both[:half], both[half:]
    j = pl.program_id(0)

    @pl.when(j == 0)
    def _():
        ka_ref[0] = top
        kb_ref[0] = low

    @pl.when(j == 1)
    def _():
        sa_ref[0] = top
        kb_ref[1] = low

    @pl.when(j == 2)
    def _():
        ka_ref[1] = top
        sb_ref[0] = low

    @pl.when(j == 3)
    def _():
        sa_ref[1] = top
        sb_ref[1] = low


def before_kernel(res_ref, ka_ref, ra_ref, za_ref, kb_ref, rb_ref, zb_ref, out_ref):
    half = res_ref.shape[0] // 2
    base_a = ka_ref[0].astype(F32) + ra_ref[0].astype(F32) + za_ref[...].astype(F32)
    base_b = kb_ref[0].astype(F32) + rb_ref[0].astype(F32) + zb_ref[...].astype(F32)
    out_ref[:half] = res_ref[:half].astype(F32) + base_a
    out_ref[half:] = res_ref[half:].astype(F32) + base_b


def final_kernel(sel_ref, ret_ref, pre_ref, out_ref):
    wide = out_ref.shape[1]
    at = pl.ds(pl.multiple_of(pl.program_id(0) * wide, wide), wide)
    delta = jnp.dot(sel_ref[...], ret_ref[:, at], preferred_element_type=F32)
    out_ref[...] = (pre_ref[...] + delta).astype(BF)


def copy_kernel(x_ref, out_ref):
    out_ref[...] = x_ref[...]


def near(v):
    return pltpu.with_memory_space_constraint(v, pltpu.VMEM)


def one_block(x, residual, weight, down, up, pool_slot, req_id, req_len):
    groups = lax.axis_size("req")
    n_t = lax.axis_size("tensor")
    me = lax.axis_index("req").astype(jnp.int32)
    t = lax.axis_index("tensor").astype(jnp.int32)
    tokens, features = x.shape
    pool = down.shape[0]
    rank = down.shape[2]
    cols = residual.shape[1]
    requests = req_len.shape[1]
    most = 2 * tokens // requests
    slots = groups * most
    half = tokens // 2
    me1 = me.reshape(1)
    t1 = t.reshape(1)
    xor = lambda m: [(i, i ^ m) for i in range(n_t)]
    sds = jax.ShapeDtypeStruct

    outgoing = pl.pallas_call(
        functools.partial(pack_kernel, pool=pool, most=most),
        out_shape=sds((slots, features), BF),
        in_specs=[SM, SM, SM, SM, VM],
        out_specs=VM,
        scratch_shapes=[pltpu.VMEM((slots, tokens), BF)],
        cost_estimate=cost(2 * slots * tokens * features, 2 * (slots + tokens) * features),
        name="pack",
    )(me1, req_len, req_id, pool_slot, x)
    arrived = lax.all_to_all(outgoing.reshape(groups, most, features), "req", split_axis=0, concat_axis=0, tiled=True)

    x, _ = lax.optimization_barrier((x, outgoing))

    def blocks(j):
        return j ^ (j >> 1)

    k = n_t // 2
    wide = 2 * tokens * features * cols * k
    to_pair = pl.pallas_call(
        pair_dot_kernel,
        out_shape=sds((k, tokens, cols), BF),
        grid_spec=pltpu.PrefetchScalarGridSpec(
            num_scalar_prefetch=1,
            grid=(k,),
            in_specs=[
                pl.BlockSpec((tokens, features), lambda j, t_ref: (0, 0)),
                pl.BlockSpec((features, cols), lambda j, t_ref: (0, t_ref[0] ^ 1 ^ (2 * blocks(j)))),
            ],
            out_specs=pl.BlockSpec((1, tokens, cols), lambda j, t_ref: (j, 0, 0)),
        ),
        cost_estimate=cost(wide, 2 * k * cols * (tokens + features)),
        name="pair_dot",
    )(t1, x, weight)
    from_pair = lax.ppermute(to_pair, "tensor", xor(1))

    piece = sds((2, half, cols), BF)
    keep = pl.BlockSpec((2, half, cols), lambda j, t_ref: (0, 0, 0))
    ka, sa, kb, sb = pl.pallas_call(
        own_dot_kernel,
        out_shape=[piece] * 4,
        grid_spec=pltpu.PrefetchScalarGridSpec(
            num_scalar_prefetch=1,
            grid=(k,),
            in_specs=[
                pl.BlockSpec((tokens, features), lambda j, t_ref: (0, 0)),
                pl.BlockSpec((features, cols), lambda j, t_ref: (0, t_ref[0] ^ (2 * blocks(j)))),
                pl.BlockSpec((1, tokens, cols), lambda j, t_ref: (j, 0, 0)),
            ],
            out_specs=[keep] * 4,
        ),
        cost_estimate=cost(wide, 2 * k * cols * (2 * tokens + features)),
        name="own_dot",
    )(t1, x, weight, from_pair)

    ids = jnp.arange(pool_slot.shape[0], dtype=jnp.int32)
    held = me * pool + jnp.arange(pool, dtype=jnp.int32)
    id_of = jnp.sum(jnp.where(pool_slot[None, :] == held[:, None], ids[None, :], 0), 1)
    uses = req_id[:, :, None] == id_of[None, None, :]
    idx = jnp.sum(jnp.where(uses, jnp.arange(pool, dtype=jnp.int32), 0), (1, 2))
    lane = jnp.arange(2 * rank, dtype=jnp.int32)
    code = jnp.broadcast_to(idx[:, None, None], (groups, most, 2 * rank)) - jnp.where(lane < rank, 0, 1)
    code = code.reshape(slots, 2 * rank)

    up_maps = pl.pallas_call(
        copy_kernel,
        out_shape=pltpu.VMEM((pool * rank, cols), BF),
        in_specs=[VM],
        out_specs=VM,
        cost_estimate=cost(0, 4 * pool * rank * cols),
        name="fetch_up",
        compiler_params=SMALL,
    )(up.reshape(pool * rank, cols))

    arrived, code, up_maps, ka, sa, kb, sb = lax.optimization_barrier(
        (arrived, code, up_maps, ka, sa, kb, sb)
    )
    code = near(code)
    pair = pltpu.VMEM((slots // 4, 2 * rank), BF)
    low = pl.pallas_call(
        functools.partial(down_kernel, pool=pool),
        out_shape=pltpu.VMEM((slots // 2, 2 * rank), BF),
        in_specs=[VM, VM, VM],
        out_specs=VM,
        cost_estimate=cost(2 * slots * pool * rank * features, 2 * slots * features),
        name="down",
        compiler_params=SMALL,
    )(
        code,
        near(arrived.reshape(slots, features)),
        near(jnp.swapaxes(down, 1, 2).reshape(pool * rank, features)),
    )
    other = lax.ppermute(low, "tensor", xor(1))
    la, lb = pl.pallas_call(
        add_split_kernel, out_shape=[pair] * 2, in_specs=[VM] * 2, out_specs=[VM] * 2, name="add_core", compiler_params=SMALL
    )(near(low), near(other))
    oa = lax.ppermute(la, "tensor", xor(2))
    ob = lax.ppermute(lb, "tensor", xor(6))
    la, lb = pl.pallas_call(
        add_kernel, out_shape=[pair] * 2, in_specs=[VM] * 4, out_specs=[VM] * 2, name="add_x", compiler_params=SMALL
    )(near(la), near(lb), near(oa), near(ob))
    oa = lax.ppermute(la, "tensor", xor(6))
    ob = lax.ppermute(lb, "tensor", xor(2))

    step = slots // 4
    raised = pl.pallas_call(
        functools.partial(up_kernel, pool=pool),
        out_shape=pltpu.HBM((slots, cols), BF),
        grid=(4,),
        in_specs=[VM] * 6,
        out_specs=pl.BlockSpec((step, cols), lambda i: (i, 0)),
        cost_estimate=cost(2 * slots * pool * rank * cols, 2 * slots * cols),
        name="up",
        compiler_params=SMALL,
    )(code, near(la), near(oa), near(lb), near(ob), near(up_maps))
    raised, sa, sb, me1 = lax.optimization_barrier((raised, sa, sb, me1))
    returned = lax.all_to_all(
        raised.reshape(groups, most, cols), "req", split_axis=0, concat_axis=0, tiled=True
    )

    sel = pl.pallas_call(
        functools.partial(unpack_matrix_kernel, pool=pool, most=most),
        out_shape=pltpu.VMEM((tokens, slots), BF),
        in_specs=[SM, SM, SM, SM],
        out_specs=VM,
        cost_estimate=cost(8 * slots * tokens, 2 * slots * tokens),
        name="unpack_matrix",
    compiler_params=SMALL,
    )(me1, req_len, req_id, pool_slot)

    ra = lax.ppermute(sa, "tensor", xor(2))
    rb = lax.ppermute(sb, "tensor", xor(6))
    za = lax.ppermute((ka[1].astype(F32) + ra[1].astype(F32)).astype(BF), "tensor", xor(6))
    zb = lax.ppermute((kb[1].astype(F32) + rb[1].astype(F32)).astype(BF), "tensor", xor(2))

    wide = cols // 4
    lead = pl.BlockSpec((1, half, wide), lambda i: (0, 0, i))
    flat = pl.BlockSpec((half, wide), lambda i: (0, i))
    tall = pl.BlockSpec((tokens, wide), lambda i: (0, i))
    pre = pl.pallas_call(
        before_kernel,
        out_shape=pltpu.HBM((tokens, cols), F32),
        grid=(4,),
        in_specs=[tall, lead, lead, flat, lead, lead, flat],
        out_specs=tall,
        cost_estimate=cost(4 * tokens * cols, 12 * tokens * cols),
        name="before",
    )(residual, ka, ra, za, kb, rb, zb)
    returned, pre, sel = lax.optimization_barrier((returned, pre, sel))
    return pl.pallas_call(
        final_kernel,
        out_shape=sds((tokens, cols), BF),
        grid=(4,),
        in_specs=[VM, VM, tall],
        out_specs=tall,
        cost_estimate=cost(2 * tokens * slots * cols, 2 * cols * (slots + 4 * tokens)),
        name="final",
        compiler_params=pltpu.CompilerParams(vmem_limit_bytes=60 * 2**20),
    )(near(sel), near(returned.reshape(slots, cols)), pre)


def solution(mesh):
    in_specs = (
        P("req", "tensor"),
        P("req", "tensor"),
        P("tensor", None),
        P("req", "tensor", None),
        P("req", None, "tensor"),
        P(),
        P(),
        P("req", None),
    )
    return jax.shard_map(one_block, mesh=mesh, in_specs=in_specs, out_specs=P("req", "tensor"), check_vma=False)
```

```python
import functools

import jax
import jax.numpy as jnp
from jax import lax
from jax.experimental import pallas as pl
from jax.experimental.pallas import tpu as pltpu
from jax.sharding import PartitionSpec as P


BF = jnp.bfloat16
F32 = jnp.float32
VM = pl.BlockSpec(memory_space=pltpu.VMEM)
SM = pl.BlockSpec(memory_space=pltpu.SMEM)


SMALL = pltpu.CompilerParams(vmem_limit_bytes=24 * 2**20)


def cost(flops, nbytes):
    return pl.CostEstimate(flops=int(flops), transcendentals=0, bytes_accessed=int(nbytes))


def pack_kernel(me_ref, len_ref, id_ref, slot_ref, x_ref, out_ref, sel_ref, *, pool, most):
    requests = len_ref.shape[1]
    tokens = x_ref.shape[0]
    rows = lax.broadcasted_iota(jnp.int32, (most, tokens), 0)
    ahead = lax.broadcasted_iota(jnp.int32, (most, tokens), 1) - rows
    me = me_ref[0]
    start = jnp.int32(0)
    for r in range(requests):
        owner = lax.div(slot_ref[id_ref[me, r]], jnp.int32(pool))
        count = len_ref[0, r]
        hit = (ahead == start) & (rows < count)
        at = pl.multiple_of(owner * most, most)
        sel_ref[pl.ds(at, most), :] = jnp.where(hit, 1.0, 0.0).astype(BF)
        start = start + count
    out_ref[...] = jnp.dot(sel_ref[...], x_ref[...], preferred_element_type=F32).astype(BF)


def unpack_matrix_kernel(me_ref, len_ref, id_ref, slot_ref, sel_ref, *, pool, most):
    requests = len_ref.shape[1]
    tokens = sel_ref.shape[0]
    lanes = 128
    per = lanes // most
    tok = lax.broadcasted_iota(jnp.int32, (tokens, lanes), 0)
    lane = lax.broadcasted_iota(jnp.int32, (tokens, lanes), 1)
    behind = tok - lane
    sel_ref[...] = jnp.zeros_like(sel_ref)
    me = me_ref[0]
    start = jnp.int32(0)
    for r in range(requests):
        owner = lax.div(slot_ref[id_ref[me, r]], jnp.int32(pool))
        count = len_ref[0, r]
        block = lax.div(owner, jnp.int32(per))
        off = (owner - block * per) * most
        hit = (behind == start - off) & (tok >= start) & (tok < start + count)
        at = pl.ds(pl.multiple_of(block * lanes, lanes), lanes)
        sel_ref[:, at] = sel_ref[:, at] + jnp.where(hit, 1.0, 0.0).astype(BF)
        start = start + count


def down_kernel(core_ref, code_ref, x_ref, d_ref, keep_ref, send_ref, *, pool):
    half, lanes = keep_ref.shape
    rank = lanes // 2
    every = lax.dot_general(x_ref[...], d_ref[...], (((1,), (1,)), ((), ())), preferred_element_type=F32)
    code = code_ref[...]
    acc = jnp.zeros(code.shape, F32)
    for b in range(pool // 2):
        acc = acc + jnp.where(code == 2 * b, every[:, 2 * b * rank:2 * (b + 1) * rank], 0.0)
    acc = acc + pltpu.roll(acc, rank, 1)
    first = lax.broadcasted_iota(jnp.int32, (half, lanes), 1) < rank
    top = jnp.where(first, acc[:half], acc[2 * half:3 * half]).astype(BF)
    low = jnp.where(first, acc[half:2 * half], acc[3 * half:]).astype(BF)
    core = core_ref[0]

    @pl.when(core == 0)
    def _():
        keep_ref[...] = top
        send_ref[...] = low

    @pl.when(core != 0)
    def _():
        keep_ref[...] = low
        send_ref[...] = top


def add_kernel(l_ref, r_ref, out_ref):
    out_ref[...] = (l_ref[...].astype(F32) + r_ref[...].astype(F32)).astype(BF)


def up_kernel(core_ref, code_ref, mine_ref, other_ref, u_ref, out_ref, *, pool):
    i = pl.program_id(0)
    rows, lanes = mine_ref.shape
    rank = lanes // 2
    own = lax.rem(i, 2) == core_ref[0]
    low = jnp.where(own, mine_ref[...].astype(F32), other_ref[...].astype(F32))
    first = lax.broadcasted_iota(jnp.int32, low.shape, 1) < rank
    low = jnp.where(jnp.logical_xor(first, i >= 2), low, pltpu.roll(low, rank, 1))
    code = code_ref[pl.ds(pl.multiple_of(i * rows, rows), rows), :]
    spread = jnp.concatenate(
        [jnp.where(code == 2 * k, low, 0.0).astype(BF) for k in range(pool // 2)], 1
    )
    out_ref[...] = jnp.dot(spread, u_ref[...], preferred_element_type=F32).astype(BF)


def pair_dot_kernel(t_ref, x_ref, w_ref, out_ref):
    out_ref[0] = jnp.dot(x_ref[...], w_ref[...], preferred_element_type=F32).astype(BF)


def own_dot_kernel(t_ref, x_ref, w_ref, p_ref, ka_ref, sa_ref, kb_ref, sb_ref):
    half = x_ref.shape[0] // 2
    both = (jnp.dot(x_ref[...], w_ref[...], preferred_element_type=F32) + p_ref[0].astype(F32)).astype(BF)
    top, low = both[:half], both[half:]
    j = pl.program_id(0)

    @pl.when(j == 0)
    def _():
        ka_ref[0] = top
        kb_ref[0] = low

    @pl.when(j == 1)
    def _():
        sa_ref[0] = top
        kb_ref[1] = low

    @pl.when(j == 2)
    def _():
        ka_ref[1] = top
        sb_ref[0] = low

    @pl.when(j == 3)
    def _():
        sa_ref[1] = top
        sb_ref[1] = low


def before_kernel(res_ref, ka_ref, ra_ref, za_ref, kb_ref, rb_ref, zb_ref, out_ref):
    half = res_ref.shape[0] // 2
    base_a = ka_ref[0].astype(F32) + ra_ref[0].astype(F32) + za_ref[...].astype(F32)
    base_b = kb_ref[0].astype(F32) + rb_ref[0].astype(F32) + zb_ref[...].astype(F32)
    out_ref[:half] = res_ref[:half].astype(F32) + base_a
    out_ref[half:] = res_ref[half:].astype(F32) + base_b


def final_kernel(sel_ref, ret_ref, pre_ref, out_ref):
    wide = out_ref.shape[1]
    at = pl.ds(pl.multiple_of(pl.program_id(0) * wide, wide), wide)
    delta = jnp.dot(sel_ref[...], ret_ref[:, at], preferred_element_type=F32)
    out_ref[...] = (pre_ref[...] + delta).astype(BF)


def copy_kernel(x_ref, out_ref):
    out_ref[...] = x_ref[...]


def near(v):
    return pltpu.with_memory_space_constraint(v, pltpu.VMEM)


def one_block(x, residual, weight, down, up, pool_slot, req_id, req_len):
    groups = lax.axis_size("req")
    n_t = lax.axis_size("tensor")
    me = lax.axis_index("req").astype(jnp.int32)
    t = lax.axis_index("tensor").astype(jnp.int32)
    tokens, features = x.shape
    pool = down.shape[0]
    rank = down.shape[2]
    cols = residual.shape[1]
    requests = req_len.shape[1]
    most = 2 * tokens // requests
    slots = groups * most
    half = tokens // 2
    me1 = me.reshape(1)
    t1 = t.reshape(1)
    xor = lambda m: [(i, i ^ m) for i in range(n_t)]
    sds = jax.ShapeDtypeStruct

    outgoing = pl.pallas_call(
        functools.partial(pack_kernel, pool=pool, most=most),
        out_shape=sds((slots, features), BF),
        in_specs=[SM, SM, SM, SM, VM],
        out_specs=VM,
        scratch_shapes=[pltpu.VMEM((slots, tokens), BF)],
        cost_estimate=cost(2 * slots * tokens * features, 2 * (slots + tokens) * features),
        name="pack",
    )(me1, req_len, req_id, pool_slot, x)
    arrived = lax.all_to_all(
        outgoing.reshape(groups, most, features), "req", split_axis=0, concat_axis=0, tiled=True
    )

    x, _ = lax.optimization_barrier((x, outgoing))

    def blocks(j):
        return j ^ (j >> 1)

    k = n_t // 2
    wide = 2 * tokens * features * cols * k
    to_pair = pl.pallas_call(
        pair_dot_kernel,
        out_shape=sds((k, tokens, cols), BF),
        grid_spec=pltpu.PrefetchScalarGridSpec(
            num_scalar_prefetch=1,
            grid=(k,),
            in_specs=[
                pl.BlockSpec((tokens, features), lambda j, t_ref: (0, 0)),
                pl.BlockSpec((features, cols), lambda j, t_ref: (0, t_ref[0] ^ 1 ^ (2 * blocks(j)))),
            ],
            out_specs=pl.BlockSpec((1, tokens, cols), lambda j, t_ref: (j, 0, 0)),
        ),
        cost_estimate=cost(wide, 2 * k * cols * (tokens + features)),
        name="pair_dot",
    )(t1, x, weight)
    from_pair = lax.ppermute(to_pair, "tensor", xor(1))

    piece = sds((2, half, cols), BF)
    keep = pl.BlockSpec((2, half, cols), lambda j, t_ref: (0, 0, 0))
    ka, sa, kb, sb = pl.pallas_call(
        own_dot_kernel,
        out_shape=[piece] * 4,
        grid_spec=pltpu.PrefetchScalarGridSpec(
            num_scalar_prefetch=1,
            grid=(k,),
            in_specs=[
                pl.BlockSpec((tokens, features), lambda j, t_ref: (0, 0)),
                pl.BlockSpec((features, cols), lambda j, t_ref: (0, t_ref[0] ^ (2 * blocks(j)))),
                pl.BlockSpec((1, tokens, cols), lambda j, t_ref: (j, 0, 0)),
            ],
            out_specs=[keep] * 4,
        ),
        cost_estimate=cost(wide, 2 * k * cols * (2 * tokens + features)),
        name="own_dot",
    )(t1, x, weight, from_pair)

    ids = jnp.arange(pool_slot.shape[0], dtype=jnp.int32)
    held = me * pool + jnp.arange(pool, dtype=jnp.int32)
    id_of = jnp.sum(jnp.where(pool_slot[None, :] == held[:, None], ids[None, :], 0), 1)
    uses = req_id[:, :, None] == id_of[None, None, :]
    idx = jnp.sum(jnp.where(uses, jnp.arange(pool, dtype=jnp.int32), 0), (1, 2))
    lane = jnp.arange(2 * rank, dtype=jnp.int32)
    code = jnp.broadcast_to(idx[:, None, None], (groups, most, 2 * rank)) - jnp.where(lane < rank, 0, 1)
    code = code.reshape(slots, 2 * rank)

    up_maps = pl.pallas_call(
        copy_kernel,
        out_shape=pltpu.VMEM((pool * rank, cols), BF),
        in_specs=[VM],
        out_specs=VM,
        cost_estimate=cost(0, 4 * pool * rank * cols),
        name="fetch_up",
        compiler_params=SMALL,
    )(up.reshape(pool * rank, cols))

    arrived, code, up_maps, ka, sa, kb, sb = lax.optimization_barrier(
        (arrived, code, up_maps, ka, sa, kb, sb)
    )
    code = near(code)
    core = t1 & 1
    piece = pltpu.VMEM((slots // 4, 2 * rank), BF)
    low, send = pl.pallas_call(
        functools.partial(down_kernel, pool=pool),
        out_shape=[piece] * 2,
        in_specs=[SM, VM, VM, VM],
        out_specs=[VM] * 2,
        cost_estimate=cost(2 * slots * pool * rank * features, 2 * slots * features),
        name="down",
        compiler_params=SMALL,
    )(
        core,
        code,
        near(arrived.reshape(slots, features)),
        near(jnp.swapaxes(down, 1, 2).reshape(pool * rank, features)),
    )
    for m, out in ((1, send), (2, None), (6, None)):
        other = lax.ppermute(low if out is None else out, "tensor", xor(m))
        low = pl.pallas_call(
            add_kernel,
            out_shape=piece,
            in_specs=[VM] * 2,
            out_specs=VM,
            name="add_low",
            compiler_params=SMALL,
        )(near(low), near(other))
    other = lax.ppermute(low, "tensor", xor(1))

    step = slots // 4
    raised = pl.pallas_call(
        functools.partial(up_kernel, pool=pool),
        out_shape=pltpu.HBM((slots, cols), BF),
        grid=(4,),
        in_specs=[SM] + [VM] * 4,
        out_specs=pl.BlockSpec((step, cols), lambda i: (i, 0)),
        cost_estimate=cost(2 * slots * pool * rank * cols, 2 * slots * cols),
        name="up",
        compiler_params=SMALL,
    )(core, code, near(low), near(other), near(up_maps))
    raised, sa, sb, me1 = lax.optimization_barrier((raised, sa, sb, me1))
    returned = lax.all_to_all(
        raised.reshape(groups, most, cols), "req", split_axis=0, concat_axis=0, tiled=True
    )

    sel = pl.pallas_call(
        functools.partial(unpack_matrix_kernel, pool=pool, most=most),
        out_shape=pltpu.VMEM((tokens, slots), BF),
        in_specs=[SM, SM, SM, SM],
        out_specs=VM,
        cost_estimate=cost(8 * slots * tokens, 2 * slots * tokens),
        name="unpack_matrix",
    compiler_params=SMALL,
    )(me1, req_len, req_id, pool_slot)

    ra = lax.ppermute(sa, "tensor", xor(2))
    rb = lax.ppermute(sb, "tensor", xor(6))
    za = lax.ppermute((ka[1].astype(F32) + ra[1].astype(F32)).astype(BF), "tensor", xor(6))
    zb = lax.ppermute((kb[1].astype(F32) + rb[1].astype(F32)).astype(BF), "tensor", xor(2))

    wide = cols // 4
    lead = pl.BlockSpec((1, half, wide), lambda i: (0, 0, i))
    flat = pl.BlockSpec((half, wide), lambda i: (0, i))
    tall = pl.BlockSpec((tokens, wide), lambda i: (0, i))
    pre = pl.pallas_call(
        before_kernel,
        out_shape=pltpu.HBM((tokens, cols), F32),
        grid=(4,),
        in_specs=[tall, lead, lead, flat, lead, lead, flat],
        out_specs=tall,
        cost_estimate=cost(4 * tokens * cols, 12 * tokens * cols),
        name="before",
    )(residual, ka, ra, za, kb, rb, zb)
    returned, pre, sel = lax.optimization_barrier((returned, pre, sel))
    return pl.pallas_call(
        final_kernel,
        out_shape=sds((tokens, cols), BF),
        grid=(4,),
        in_specs=[VM, VM, tall],
        out_specs=tall,
        cost_estimate=cost(2 * tokens * slots * cols, 2 * cols * (slots + 4 * tokens)),
        name="final",
        compiler_params=pltpu.CompilerParams(vmem_limit_bytes=59 * 2**20),
    )(near(sel), near(returned.reshape(slots, cols)), pre)


def solution(mesh):
    in_specs = (
        P("req", "tensor"),
        P("req", "tensor"),
        P("tensor", None),
        P("req", "tensor", None),
        P("req", None, "tensor"),
        P(),
        P(),
        P("req", None),
    )
    return jax.shard_map(
        one_block, mesh=mesh, in_specs=in_specs, out_specs=P("req", "tensor"), check_vma=False
    )
```

```python
import functools

import jax
import jax.numpy as jnp
from jax import lax
from jax.experimental import pallas as pl
from jax.experimental.pallas import tpu as pltpu
from jax.sharding import PartitionSpec as P


BF = jnp.bfloat16
F32 = jnp.float32
VM = pl.BlockSpec(memory_space=pltpu.VMEM)
SM = pl.BlockSpec(memory_space=pltpu.SMEM)


SMALL = pltpu.CompilerParams(vmem_limit_bytes=24 * 2**20)


def cost(flops, nbytes):
    return pl.CostEstimate(flops=int(flops), transcendentals=0, bytes_accessed=int(nbytes))


def pack_kernel(me_ref, len_ref, id_ref, slot_ref, x_ref, out_ref, sel_ref, *, pool, most):
    requests = len_ref.shape[1]
    tokens = x_ref.shape[0]
    rows = lax.broadcasted_iota(jnp.int32, (most, tokens), 0)
    ahead = lax.broadcasted_iota(jnp.int32, (most, tokens), 1) - rows
    me = me_ref[0]
    start = jnp.int32(0)
    for r in range(requests):
        owner = lax.div(slot_ref[id_ref[me, r]], jnp.int32(pool))
        at = pl.multiple_of(owner * most, most)
        sel_ref[pl.ds(at, most), :] = jnp.where(ahead == start, 1.0, 0.0).astype(BF)
        start = start + len_ref[0, r]
    out_ref[...] = jnp.dot(sel_ref[...], x_ref[...], preferred_element_type=F32).astype(BF)


def unpack_matrix_kernel(me_ref, len_ref, id_ref, slot_ref, sel_ref, *, pool, most):
    requests = len_ref.shape[1]
    tokens = sel_ref.shape[0]
    lanes = 128
    per = lanes // most
    tok = lax.broadcasted_iota(jnp.int32, (tokens, lanes), 0)
    lane = lax.broadcasted_iota(jnp.int32, (tokens, lanes), 1)
    behind = tok - lane
    sel_ref[...] = jnp.zeros_like(sel_ref)
    me = me_ref[0]
    start = jnp.int32(0)
    for r in range(requests):
        owner = lax.div(slot_ref[id_ref[me, r]], jnp.int32(pool))
        count = len_ref[0, r]
        block = lax.div(owner, jnp.int32(per))
        off = (owner - block * per) * most
        hit = (behind == start - off) & (tok >= start) & (tok < start + count)
        at = pl.ds(pl.multiple_of(block * lanes, lanes), lanes)
        sel_ref[:, at] = sel_ref[:, at] + jnp.where(hit, 1.0, 0.0).astype(BF)
        start = start + count


def down_kernel(core_ref, code_ref, x_ref, d_ref, keep_ref, send_ref, *, pool):
    half, lanes = keep_ref.shape
    rank = lanes // 2
    every = lax.dot_general(x_ref[...], d_ref[...], (((1,), (1,)), ((), ())), preferred_element_type=F32)
    code = code_ref[...]
    acc = jnp.zeros(code.shape, F32)
    for b in range(pool // 2):
        acc = acc + jnp.where(code == 2 * b, every[:, 2 * b * rank:2 * (b + 1) * rank], 0.0)
    acc = acc + pltpu.roll(acc, rank, 1)
    first = lax.broadcasted_iota(jnp.int32, (half, lanes), 1) < rank
    top = jnp.where(first, acc[:half], acc[2 * half:3 * half]).astype(BF)
    low = jnp.where(first, acc[half:2 * half], acc[3 * half:]).astype(BF)
    core = core_ref[0]

    @pl.when(core == 0)
    def _():
        keep_ref[...] = top
        send_ref[...] = low

    @pl.when(core != 0)
    def _():
        keep_ref[...] = low
        send_ref[...] = top


def up_kernel(core_ref, code_ref, mine_ref, other_ref, u_ref, out_ref, *, pool):
    i = pl.program_id(0)
    rows, lanes = mine_ref.shape
    rank = lanes // 2
    own = lax.rem(i, 2) == core_ref[0]
    low = jnp.where(own, mine_ref[...].astype(F32), other_ref[...].astype(F32))
    first = lax.broadcasted_iota(jnp.int32, low.shape, 1) < rank
    low = jnp.where(jnp.logical_xor(first, i >= 2), low, pltpu.roll(low, rank, 1))
    code = code_ref[pl.ds(pl.multiple_of(i * rows, rows), rows), :]
    spread = jnp.concatenate(
        [jnp.where(code == 2 * k, low, 0.0).astype(BF) for k in range(pool // 2)], 1
    )
    out_ref[...] = jnp.dot(spread, u_ref[...], preferred_element_type=F32).astype(BF)


def pair_dot_kernel(t_ref, x_ref, w_ref, out_ref):
    out_ref[0] = jnp.dot(x_ref[...], w_ref[...], preferred_element_type=F32).astype(BF)


def own_dot_kernel(t_ref, x_ref, w_ref, p_ref, a0_ref, b0_ref, a1_ref, b1_ref):
    half = x_ref.shape[0] // 2
    both = (jnp.dot(x_ref[...], w_ref[...], preferred_element_type=F32) + p_ref[0].astype(F32)).astype(BF)
    j = pl.program_id(0)

    @pl.when(j == 0)
    def _():
        a0_ref[...] = both[:half]
        b0_ref[...] = both[half:]

    @pl.when(j == 1)
    def _():
        a1_ref[...] = both[:half]
        b1_ref[...] = both[half:]


def before_kernel(res_ref, ka_ref, ra_ref, kb_ref, rb_ref, out_ref):
    half = res_ref.shape[0] // 2
    out_ref[:half] = res_ref[:half].astype(F32) + (ka_ref[...].astype(F32) + ra_ref[...].astype(F32))
    out_ref[half:] = res_ref[half:].astype(F32) + (kb_ref[...].astype(F32) + rb_ref[...].astype(F32))


def final_kernel(sel_ref, ret_ref, pre_ref, za_ref, zb_ref, out_ref):
    wide = out_ref.shape[1]
    half = za_ref.shape[0]
    at = pl.ds(pl.multiple_of(pl.program_id(0) * wide, wide), wide)
    delta = jnp.dot(sel_ref[...], ret_ref[:, at], preferred_element_type=F32) + pre_ref[...]
    out_ref[:half] = (delta[:half] + za_ref[...].astype(F32)).astype(BF)
    out_ref[half:] = (delta[half:] + zb_ref[...].astype(F32)).astype(BF)


def sum_kernel(*refs):
    acc = refs[0][...].astype(F32)
    for r in refs[1:-1]:
        acc = acc + r[...].astype(F32)
    refs[-1][...] = acc.astype(BF)


def copy_kernel(x_ref, out_ref):
    out_ref[...] = x_ref[...]


def near(v):
    return pltpu.with_memory_space_constraint(v, pltpu.VMEM)


def one_block(x, residual, weight, down, up, pool_slot, req_id, req_len):
    groups = lax.axis_size("req")
    n_t = lax.axis_size("tensor")
    me = lax.axis_index("req").astype(jnp.int32)
    t = lax.axis_index("tensor").astype(jnp.int32)
    tokens, features = x.shape
    pool = down.shape[0]
    rank = down.shape[2]
    cols = residual.shape[1]
    requests = req_len.shape[1]
    most = 2 * tokens // requests
    slots = groups * most
    half = tokens // 2
    me1 = me.reshape(1)
    t1 = t.reshape(1)
    xor = lambda m: [(i, i ^ m) for i in range(n_t)]
    sds = jax.ShapeDtypeStruct

    outgoing = pl.pallas_call(
        functools.partial(pack_kernel, pool=pool, most=most),
        out_shape=sds((slots, features), BF),
        in_specs=[SM, SM, SM, SM, VM],
        out_specs=VM,
        scratch_shapes=[pltpu.VMEM((slots, tokens), BF)],
        cost_estimate=cost(2 * slots * tokens * features, 2 * (slots + tokens) * features),
        name="pack",
    )(me1, req_len, req_id, pool_slot, x)
    arrived = lax.all_to_all(outgoing.reshape(groups, most, features), "req", split_axis=0, concat_axis=0, tiled=True)

    def parts(offsets, x):
        def order(j):
            return jnp.where(j == 0, offsets[0], offsets[1])

        n = len(offsets)
        flops = 2 * tokens * features * cols * n
        whole = pl.BlockSpec((tokens, features), lambda j, t_ref: (0, 0))
        out = pl.pallas_call(
            pair_dot_kernel,
            out_shape=sds((n, tokens, cols), BF),
            grid_spec=pltpu.PrefetchScalarGridSpec(
                num_scalar_prefetch=1,
                grid=(n,),
                in_specs=[whole, pl.BlockSpec((features, cols), lambda j, t_ref: (0, t_ref[0] ^ 1 ^ (2 * order(j))))],
                out_specs=pl.BlockSpec((1, tokens, cols), lambda j, t_ref: (j, 0, 0)),
            ),
            cost_estimate=cost(flops, 2 * n * cols * (tokens + features)),
            name="pair_dot",
        )(t1, x, weight)

        def own(x, came):
            piece = sds((half, cols), BF)
            keep = pl.BlockSpec((half, cols), lambda j, t_ref: (0, 0))
            return pl.pallas_call(
                own_dot_kernel,
                out_shape=[piece] * 4,
                grid_spec=pltpu.PrefetchScalarGridSpec(
                    num_scalar_prefetch=1,
                    grid=(n,),
                    in_specs=[
                        whole,
                        pl.BlockSpec((features, cols), lambda j, t_ref: (0, t_ref[0] ^ (2 * order(j)))),
                        pl.BlockSpec((1, tokens, cols), lambda j, t_ref: (j, 0, 0)),
                    ],
                    out_specs=[keep] * 4,
                ),
                cost_estimate=cost(flops, 2 * n * cols * (2 * tokens + features)),
                name="own_dot",
            )(t1, x, weight, came)

        return out, own

    x, _ = lax.optimization_barrier((x, outgoing))
    to_1, own_1 = parts((2, 1), x)
    from_1 = lax.ppermute(to_1, "tensor", xor(1))
    x, _ = lax.optimization_barrier((x, to_1))
    to_2, own_2 = parts((3, 0), x)
    from_2 = lax.ppermute(to_2, "tensor", xor(1))
    x, _ = lax.optimization_barrier((x, to_2))
    s2a, s2b, s1a, k1b = own_1(x, from_1)
    r2a = lax.ppermute(s2a, "tensor", xor(2))
    r2b = lax.ppermute(s2b, "tensor", xor(6))
    x, _ = lax.optimization_barrier((x, s2a))
    k3a, s3b, k0a, k0b = own_2(x, from_2)

    ids = jnp.arange(pool_slot.shape[0], dtype=jnp.int32)
    held = me * pool + jnp.arange(pool, dtype=jnp.int32)
    id_of = jnp.sum(jnp.where(pool_slot[None, :] == held[:, None], ids[None, :], 0), 1)
    uses = req_id[:, :, None] == id_of[None, None, :]
    idx = jnp.sum(jnp.where(uses, jnp.arange(pool, dtype=jnp.int32), 0), (1, 2))
    lane = jnp.arange(2 * rank, dtype=jnp.int32)
    code = jnp.broadcast_to(idx[:, None, None], (groups, most, 2 * rank)) - jnp.where(lane < rank, 0, 1)
    code = code.reshape(slots, 2 * rank)

    up_maps = pl.pallas_call(
        copy_kernel,
        out_shape=pltpu.VMEM((pool * rank, cols), BF),
        in_specs=[VM],
        out_specs=VM,
        cost_estimate=cost(0, 4 * pool * rank * cols),
        name="fetch_up",
        compiler_params=SMALL,
    )(up.reshape(pool * rank, cols))

    arrived, code, up_maps, k0a, s3b = lax.optimization_barrier((arrived, code, up_maps, k0a, s3b))
    code = near(code)
    core = t1 & 1
    piece = pltpu.VMEM((slots // 4, 2 * rank), BF)
    low, send = pl.pallas_call(
        functools.partial(down_kernel, pool=pool),
        out_shape=[piece] * 2,
        in_specs=[SM, VM, VM, VM],
        out_specs=[VM] * 2,
        cost_estimate=cost(2 * slots * pool * rank * features, 2 * slots * features),
        name="down",
        compiler_params=SMALL,
    )(
        core,
        code,
        near(arrived.reshape(slots, features)),
        near(jnp.swapaxes(down, 1, 2).reshape(pool * rank, features)),
    )

    def total(*terms):
        return pl.pallas_call(
            sum_kernel,
            out_shape=piece,
            in_specs=[VM] * len(terms),
            out_specs=VM,
            name="sum_low",
            compiler_params=SMALL,
        )(*[near(v) for v in terms])

    low = total(low, lax.ppermute(send, "tensor", xor(1)))
    low = total(low, *[lax.ppermute(low, "tensor", xor(m)) for m in (4, 2, 6)])
    other = lax.ppermute(low, "tensor", xor(1))

    step = slots // 4
    raised = pl.pallas_call(
        functools.partial(up_kernel, pool=pool),
        out_shape=pltpu.HBM((slots, cols), BF),
        grid=(4,),
        in_specs=[SM] + [VM] * 4,
        out_specs=pl.BlockSpec((step, cols), lambda i: (i, 0)),
        cost_estimate=cost(2 * slots * pool * rank * cols, 2 * slots * cols),
        name="up",
        compiler_params=SMALL,
    )(core, code, near(low), near(other), near(up_maps))
    raised, s1a, s3b, k3a, k1b, me1 = lax.optimization_barrier((raised, s1a, s3b, k3a, k1b, me1))
    returned = lax.all_to_all(
        raised.reshape(groups, most, cols), "req", split_axis=0, concat_axis=0, tiled=True
    )

    sel = pl.pallas_call(
        functools.partial(unpack_matrix_kernel, pool=pool, most=most),
        out_shape=pltpu.VMEM((tokens, slots), BF),
        in_specs=[SM, SM, SM, SM],
        out_specs=VM,
        cost_estimate=cost(8 * slots * tokens, 2 * slots * tokens),
        name="unpack_matrix",
    compiler_params=SMALL,
    )(me1, req_len, req_id, pool_slot)

    za = lax.ppermute((k3a.astype(F32) + r2a.astype(F32)).astype(BF), "tensor", xor(6))
    zb = lax.ppermute((k1b.astype(F32) + r2b.astype(F32)).astype(BF), "tensor", xor(2))
    r1a = lax.ppermute(s1a, "tensor", xor(2))
    r3b = lax.ppermute(s3b, "tensor", xor(6))

    wide = cols // 4
    flat = pl.BlockSpec((half, wide), lambda i: (0, i))
    tall = pl.BlockSpec((tokens, wide), lambda i: (0, i))
    pre = pl.pallas_call(
        before_kernel,
        out_shape=pltpu.HBM((tokens, cols), F32),
        grid=(4,),
        in_specs=[tall, flat, flat, flat, flat],
        out_specs=tall,
        cost_estimate=cost(4 * tokens * cols, 12 * tokens * cols),
        name="before",
    )(residual, k0a, r1a, k0b, r3b)
    returned, pre, sel, za, zb = lax.optimization_barrier((returned, pre, sel, za, zb))
    return pl.pallas_call(
        final_kernel,
        out_shape=sds((tokens, cols), BF),
        grid=(4,),
        in_specs=[VM, VM, tall, flat, flat],
        out_specs=tall,
        cost_estimate=cost(2 * tokens * slots * cols, 2 * cols * (slots + 4 * tokens)),
        name="final",
        compiler_params=pltpu.CompilerParams(vmem_limit_bytes=59 * 2**20),
    )(near(sel), near(returned.reshape(slots, cols)), pre, za, zb)


def solution(mesh):
    in_specs = (
        P("req", "tensor"),
        P("req", "tensor"),
        P("tensor", None),
        P("req", "tensor", None),
        P("req", None, "tensor"),
        P(),
        P(),
        P("req", None),
    )
    return jax.shard_map(one_block, mesh=mesh, in_specs=in_specs, out_specs=P("req", "tensor"), check_vma=False)
```

```python
import functools

import jax
import jax.numpy as jnp
from jax import lax
from jax.experimental import pallas as pl
from jax.experimental.pallas import tpu as pltpu
from jax.sharding import PartitionSpec as P


BF = jnp.bfloat16
F32 = jnp.float32
VM = pl.BlockSpec(memory_space=pltpu.VMEM)
SM = pl.BlockSpec(memory_space=pltpu.SMEM)
HB = pl.BlockSpec(memory_space=pl.ANY)
DMA = pltpu.SemaphoreType.DMA
PARTS = 4


SMALL = pltpu.CompilerParams(vmem_limit_bytes=24 * 2**20)


def cost(flops, nbytes):
    return pl.CostEstimate(flops=int(flops), transcendentals=0, bytes_accessed=int(nbytes))


def pack_kernel(me_ref, len_ref, id_ref, slot_ref, x_ref, out_ref, x_buf, sel_ref, o_buf, x_sem, o_sem, *, pool, most):
    fetch = pltpu.make_async_copy(x_ref, x_buf, x_sem)
    fetch.start()
    requests = len_ref.shape[1]
    tokens = x_ref.shape[0]
    rows = lax.broadcasted_iota(jnp.int32, (most, tokens), 0)
    ahead = lax.broadcasted_iota(jnp.int32, (most, tokens), 1) - rows
    me = me_ref[0]
    start = jnp.int32(0)
    for r in range(requests):
        owner = lax.div(slot_ref[id_ref[me, r]], jnp.int32(pool))
        at = pl.multiple_of(owner * most, most)
        sel_ref[pl.ds(at, most), :] = jnp.where(ahead == start, 1.0, 0.0).astype(BF)
        start = start + len_ref[0, r]
    fetch.wait()
    n = out_ref.shape[0] // PARTS
    leaving = []
    for i in range(PARTS):
        at = pl.ds(i * n, n)
        o_buf[at, :] = jnp.dot(sel_ref[at, :], x_buf[...], preferred_element_type=F32).astype(BF)
        leaving.append(pltpu.make_async_copy(o_buf.at[at], out_ref.at[at], o_sem.at[i]))
        leaving[-1].start()
    for copy in leaving:
        copy.wait()


def unpack_matrix_kernel(me_ref, len_ref, id_ref, slot_ref, sel_ref, *, pool, most):
    requests = len_ref.shape[1]
    tokens = sel_ref.shape[0]
    lanes = 128
    per = lanes // most
    tok = lax.broadcasted_iota(jnp.int32, (tokens, lanes), 0)
    lane = lax.broadcasted_iota(jnp.int32, (tokens, lanes), 1)
    behind = tok - lane
    sel_ref[...] = jnp.zeros_like(sel_ref)
    me = me_ref[0]
    start = jnp.int32(0)
    for r in range(requests):
        owner = lax.div(slot_ref[id_ref[me, r]], jnp.int32(pool))
        count = len_ref[0, r]
        block = lax.div(owner, jnp.int32(per))
        off = (owner - block * per) * most
        hit = (behind == start - off) & (tok >= start) & (tok < start + count)
        at = pl.ds(pl.multiple_of(block * lanes, lanes), lanes)
        sel_ref[:, at] = sel_ref[:, at] + jnp.where(hit, 1.0, 0.0).astype(BF)
        start = start + count


def down_kernel(core_ref, code_ref, x_ref, d_ref, keep_ref, send_ref, *, pool):
    half, lanes = keep_ref.shape
    rank = lanes // 2
    every = lax.dot_general(x_ref[...], d_ref[...], (((1,), (1,)), ((), ())), preferred_element_type=F32)
    code = code_ref[...]
    acc = jnp.zeros(code.shape, F32)
    for b in range(pool // 2):
        acc = acc + jnp.where(code == 2 * b, every[:, 2 * b * rank:2 * (b + 1) * rank], 0.0)
    acc = acc + pltpu.roll(acc, rank, 1)
    first = lax.broadcasted_iota(jnp.int32, (half, lanes), 1) < rank
    top = jnp.where(first, acc[:half], acc[2 * half:3 * half]).astype(BF)
    low = jnp.where(first, acc[half:2 * half], acc[3 * half:]).astype(BF)
    core = core_ref[0]

    @pl.when(core == 0)
    def _():
        keep_ref[...] = top
        send_ref[...] = low

    @pl.when(core != 0)
    def _():
        keep_ref[...] = low
        send_ref[...] = top


def up_kernel(core_ref, code_ref, low_ref, u_ref, *rest, pool, flip):
    out_ref, o_buf, o_sem = rest[-3:]
    rows, lanes = low_ref.shape
    rank = lanes // 2
    which = core_ref[0] ^ flip
    packed = low_ref[...].astype(F32)
    turned = pltpu.roll(packed, rank, 1)
    first = lax.broadcasted_iota(jnp.int32, packed.shape, 1) < rank
    leaving = []
    for i in range(2):
        low = jnp.where(first, packed, turned) if i == 0 else jnp.where(first, turned, packed)
        at = pl.ds(pl.multiple_of((2 * i + which) * rows, rows), rows)
        code = code_ref[at, :]
        spread = jnp.concatenate(
            [jnp.where(code == 2 * k, low, 0.0).astype(BF) for k in range(pool // 2)], 1
        )
        o_buf[i] = jnp.dot(spread, u_ref[...], preferred_element_type=F32).astype(BF)
        leaving.append(pltpu.make_async_copy(o_buf.at[i], out_ref.at[at], o_sem.at[i]))
        leaving[-1].start()
    for copy in leaving:
        copy.wait()


def pair_dot_kernel(t_ref, x_ref, w_ref, out_ref):
    out_ref[0] = jnp.dot(x_ref[...], w_ref[...], preferred_element_type=F32).astype(BF)


def own_dot_kernel(t_ref, x_ref, w_ref, p_ref, a0_ref, b0_ref, a1_ref, b1_ref):
    half = x_ref.shape[0] // 2
    both = (jnp.dot(x_ref[...], w_ref[...], preferred_element_type=F32) + p_ref[0].astype(F32)).astype(BF)
    j = pl.program_id(0)

    @pl.when(j == 0)
    def _():
        a0_ref[...] = both[:half]
        b0_ref[...] = both[half:]

    @pl.when(j == 1)
    def _():
        a1_ref[...] = both[:half]
        b1_ref[...] = both[half:]


def before_kernel(res_ref, ka_ref, ra_ref, za_ref, kb_ref, rb_ref, zb_ref, out_ref):
    half = res_ref.shape[0] // 2
    base_a = ka_ref[...].astype(F32) + ra_ref[...].astype(F32) + za_ref[...].astype(F32)
    base_b = kb_ref[...].astype(F32) + rb_ref[...].astype(F32) + zb_ref[...].astype(F32)
    out_ref[:half] = res_ref[:half].astype(F32) + base_a
    out_ref[half:] = res_ref[half:].astype(F32) + base_b


def final_kernel(sel_ref, ret_ref, pre_ref, out_ref, p_buf, o_buf, p_sem, o_sem):
    n = out_ref.shape[1] // PARTS
    at = [pl.ds(i * n, n) for i in range(PARTS)]
    coming = [pltpu.make_async_copy(pre_ref.at[:, at[i]], p_buf.at[i], p_sem.at[i]) for i in range(PARTS)]
    leaving = [pltpu.make_async_copy(o_buf.at[i], out_ref.at[:, at[i]], o_sem.at[i]) for i in range(PARTS)]
    for copy in coming:
        copy.start()
    for i in range(PARTS):
        delta = jnp.dot(sel_ref[...], ret_ref[:, at[i]], preferred_element_type=F32)
        coming[i].wait()
        o_buf[i] = (p_buf[i] + delta).astype(BF)
        leaving[i].start()
    for copy in leaving:
        copy.wait()


def sum_kernel(*refs):
    acc = refs[0][...].astype(F32)
    for r in refs[1:-1]:
        acc = acc + r[...].astype(F32)
    refs[-1][...] = acc.astype(BF)


def copy_kernel(x_ref, out_ref):
    out_ref[...] = x_ref[...]


def near(v):
    return pltpu.with_memory_space_constraint(v, pltpu.VMEM)


def one_block(x, residual, weight, down, up, pool_slot, req_id, req_len):
    groups = lax.axis_size("req")
    n_t = lax.axis_size("tensor")
    me = lax.axis_index("req").astype(jnp.int32)
    t = lax.axis_index("tensor").astype(jnp.int32)
    tokens, features = x.shape
    pool = down.shape[0]
    rank = down.shape[2]
    cols = residual.shape[1]
    requests = req_len.shape[1]
    most = 2 * tokens // requests
    slots = groups * most
    half = tokens // 2
    me1 = me.reshape(1)
    t1 = t.reshape(1)
    xor = lambda m: [(i, i ^ m) for i in range(n_t)]
    sds = jax.ShapeDtypeStruct

    outgoing = pl.pallas_call(
        functools.partial(pack_kernel, pool=pool, most=most),
        out_shape=sds((slots, features), BF),
        in_specs=[SM, SM, SM, SM, HB],
        out_specs=HB,
        scratch_shapes=[
            pltpu.VMEM((tokens, features), BF),
            pltpu.VMEM((slots, tokens), BF),
            pltpu.VMEM((slots, features), BF),
            DMA,
            DMA((PARTS,)),
        ],
        cost_estimate=cost(2 * slots * tokens * features, 2 * (slots + tokens) * features),
        name="pack",
    )(me1, req_len, req_id, pool_slot, x)
    arrived = lax.all_to_all(outgoing.reshape(groups, most, features), "req", split_axis=0, concat_axis=0, tiled=True)

    def parts(offsets, x):
        def order(j):
            return jnp.where(j == 0, offsets[0], offsets[1])

        n = len(offsets)
        flops = 2 * tokens * features * cols * n
        whole = pl.BlockSpec((tokens, features), lambda j, t_ref: (0, 0))
        out = pl.pallas_call(
            pair_dot_kernel,
            out_shape=sds((n, tokens, cols), BF),
            grid_spec=pltpu.PrefetchScalarGridSpec(
                num_scalar_prefetch=1,
                grid=(n,),
                in_specs=[whole, pl.BlockSpec((features, cols), lambda j, t_ref: (0, t_ref[0] ^ 1 ^ (2 * order(j))))],
                out_specs=pl.BlockSpec((1, tokens, cols), lambda j, t_ref: (j, 0, 0)),
            ),
            cost_estimate=cost(flops, 2 * n * cols * (tokens + features)),
            name="pair_dot",
        )(t1, x, weight)

        def own(x, came):
            piece = sds((half, cols), BF)
            keep = pl.BlockSpec((half, cols), lambda j, t_ref: (0, 0))
            return pl.pallas_call(
                own_dot_kernel,
                out_shape=[piece] * 4,
                grid_spec=pltpu.PrefetchScalarGridSpec(
                    num_scalar_prefetch=1,
                    grid=(n,),
                    in_specs=[
                        whole,
                        pl.BlockSpec((features, cols), lambda j, t_ref: (0, t_ref[0] ^ (2 * order(j)))),
                        pl.BlockSpec((1, tokens, cols), lambda j, t_ref: (j, 0, 0)),
                    ],
                    out_specs=[keep] * 4,
                ),
                cost_estimate=cost(flops, 2 * n * cols * (2 * tokens + features)),
                name="own_dot",
            )(t1, x, weight, came)

        return out, own

    x, _ = lax.optimization_barrier((x, outgoing))
    to_1, own_1 = parts((2, 1), x)
    from_1 = lax.ppermute(to_1, "tensor", xor(1))
    x, _ = lax.optimization_barrier((x, to_1))
    to_2, own_2 = parts((3, 0), x)
    from_2 = lax.ppermute(to_2, "tensor", xor(1))
    x, _ = lax.optimization_barrier((x, to_2))
    s2a, s2b, s1a, k1b = own_1(x, from_1)
    r2a = lax.ppermute(s2a, "tensor", xor(2))
    r2b = lax.ppermute(s2b, "tensor", xor(6))
    x, _ = lax.optimization_barrier((x, s2a))
    k3a, s3b, k0a, k0b = own_2(x, from_2)

    ids = jnp.arange(pool_slot.shape[0], dtype=jnp.int32)
    held = me * pool + jnp.arange(pool, dtype=jnp.int32)
    id_of = jnp.sum(jnp.where(pool_slot[None, :] == held[:, None], ids[None, :], 0), 1)
    uses = req_id[:, :, None] == id_of[None, None, :]
    idx = jnp.sum(jnp.where(uses, jnp.arange(pool, dtype=jnp.int32), 0), (1, 2))
    lane = jnp.arange(2 * rank, dtype=jnp.int32)
    code = jnp.broadcast_to(idx[:, None, None], (groups, most, 2 * rank)) - jnp.where(lane < rank, 0, 1)
    code = code.reshape(slots, 2 * rank)

    up_maps = pl.pallas_call(
        copy_kernel,
        out_shape=pltpu.VMEM((pool * rank, cols), BF),
        in_specs=[VM],
        out_specs=VM,
        cost_estimate=cost(0, 4 * pool * rank * cols),
        name="fetch_up",
        compiler_params=SMALL,
    )(up.reshape(pool * rank, cols))

    arrived, code, up_maps, k0a, s3b = lax.optimization_barrier((arrived, code, up_maps, k0a, s3b))
    code = near(code)
    core = t1 & 1
    piece = pltpu.VMEM((slots // 4, 2 * rank), BF)
    low, send = pl.pallas_call(
        functools.partial(down_kernel, pool=pool),
        out_shape=[piece] * 2,
        in_specs=[SM, VM, VM, VM],
        out_specs=[VM] * 2,
        cost_estimate=cost(2 * slots * pool * rank * features, 2 * slots * features),
        name="down",
        compiler_params=SMALL,
    )(
        core,
        code,
        near(arrived.reshape(slots, features)),
        near(jnp.swapaxes(down, 1, 2).reshape(pool * rank, features)),
    )

    def total(*terms):
        return pl.pallas_call(
            sum_kernel,
            out_shape=piece,
            in_specs=[VM] * len(terms),
            out_specs=VM,
            name="sum_low",
            compiler_params=SMALL,
        )(*[near(v) for v in terms])

    low = total(low, lax.ppermute(send, "tensor", xor(1)))
    low = total(low, *[lax.ppermute(low, "tensor", xor(m)) for m in (4, 2, 6)])
    other = lax.ppermute(low, "tensor", xor(1))

    def lift(rows_low, flip, filled=()):
        return pl.pallas_call(
            functools.partial(up_kernel, pool=pool, flip=flip),
            out_shape=pltpu.HBM((slots, cols), BF),
            in_specs=[SM, VM, VM, VM] + [HB] * len(filled),
            out_specs=HB,
            scratch_shapes=[pltpu.VMEM((2, slots // 4, cols), BF), DMA((2,))],
            input_output_aliases={4: 0} if filled else {},
            cost_estimate=cost(slots * pool * rank * cols, slots * cols),
            name="up",
            compiler_params=SMALL,
        )(core, code, near(rows_low), near(up_maps), *filled)

    raised = lift(low, 0)
    raised = lift(other, 1, (raised,))
    raised, s1a, s3b, k3a, k1b, me1 = lax.optimization_barrier((raised, s1a, s3b, k3a, k1b, me1))
    returned = lax.all_to_all(
        raised.reshape(groups, most, cols), "req", split_axis=0, concat_axis=0, tiled=True
    )

    sel = pl.pallas_call(
        functools.partial(unpack_matrix_kernel, pool=pool, most=most),
        out_shape=pltpu.VMEM((tokens, slots), BF),
        in_specs=[SM, SM, SM, SM],
        out_specs=VM,
        cost_estimate=cost(8 * slots * tokens, 2 * slots * tokens),
        name="unpack_matrix",
    compiler_params=SMALL,
    )(me1, req_len, req_id, pool_slot)

    za = lax.ppermute((k3a.astype(F32) + r2a.astype(F32)).astype(BF), "tensor", xor(6))
    zb = lax.ppermute((k1b.astype(F32) + r2b.astype(F32)).astype(BF), "tensor", xor(2))
    r1a = lax.ppermute(s1a, "tensor", xor(2))
    r3b = lax.ppermute(s3b, "tensor", xor(6))

    wide = cols // 4
    flat = pl.BlockSpec((half, wide), lambda i: (0, i))
    tall = pl.BlockSpec((tokens, wide), lambda i: (0, i))
    pre = pl.pallas_call(
        before_kernel,
        out_shape=pltpu.HBM((tokens, cols), F32),
        grid=(4,),
        in_specs=[tall] + [flat] * 6,
        out_specs=tall,
        cost_estimate=cost(4 * tokens * cols, 12 * tokens * cols),
        name="before",
    )(residual, k0a, r1a, za, k0b, r3b, zb)
    returned, pre, sel = lax.optimization_barrier((returned, pre, sel))
    return pl.pallas_call(
        final_kernel,
        out_shape=sds((tokens, cols), BF),
        in_specs=[VM, VM, HB],
        out_specs=HB,
        scratch_shapes=[
            pltpu.VMEM((PARTS, tokens, cols // PARTS), F32),
            pltpu.VMEM((PARTS, tokens, cols // PARTS), BF),
            DMA((PARTS,)),
            DMA((PARTS,)),
        ],
        cost_estimate=cost(2 * tokens * slots * cols, 2 * cols * (slots + 4 * tokens)),
        name="final",
        compiler_params=pltpu.CompilerParams(vmem_limit_bytes=59 * 2**20),
    )(near(sel), near(returned.reshape(slots, cols)), pre)


def solution(mesh):
    in_specs = (
        P("req", "tensor"),
        P("req", "tensor"),
        P("tensor", None),
        P("req", "tensor", None),
        P("req", None, "tensor"),
        P(),
        P(),
        P("req", None),
    )
    return jax.shard_map(one_block, mesh=mesh, in_specs=in_specs, out_specs=P("req", "tensor"), check_vma=False)
```

```python
import functools

import jax
import jax.numpy as jnp
from jax import lax
from jax.experimental import pallas as pl
from jax.experimental.pallas import tpu as pltpu
from jax.sharding import PartitionSpec as P


BF = jnp.bfloat16
F32 = jnp.float32
VM = pl.BlockSpec(memory_space=pltpu.VMEM)
SM = pl.BlockSpec(memory_space=pltpu.SMEM)
HB = pl.BlockSpec(memory_space=pl.ANY)
DMA = pltpu.SemaphoreType.DMA
PARTS = 4


SMALL = pltpu.CompilerParams(vmem_limit_bytes=24 * 2**20)


def cost(flops, nbytes):
    return pl.CostEstimate(flops=int(flops), transcendentals=0, bytes_accessed=int(nbytes))


def pack_kernel(me_ref, len_ref, id_ref, slot_ref, x_ref, out_ref, sel_ref, *, pool, most):
    requests = len_ref.shape[1]
    tokens = x_ref.shape[0]
    rows = lax.broadcasted_iota(jnp.int32, (most, tokens), 0)
    ahead = lax.broadcasted_iota(jnp.int32, (most, tokens), 1) - rows
    me = me_ref[0]
    start = jnp.int32(0)
    for r in range(requests):
        owner = lax.div(slot_ref[id_ref[me, r]], jnp.int32(pool))
        at = pl.multiple_of(owner * most, most)
        sel_ref[pl.ds(at, most), :] = jnp.where(ahead == start, 1.0, 0.0).astype(BF)
        start = start + len_ref[0, r]
    out_ref[...] = jnp.dot(sel_ref[...], x_ref[...], preferred_element_type=F32).astype(BF)


def unpack_index_kernel(me_ref, len_ref, id_ref, slot_ref, out_ref, *, pool, most):
    tok = lax.broadcasted_iota(jnp.int32, out_ref.shape, 0)
    me = me_ref[0]
    start = jnp.int32(0)
    shift = jnp.zeros(out_ref.shape, jnp.int32)
    for r in range(len_ref.shape[1]):
        owner = lax.div(slot_ref[id_ref[me, r]], jnp.int32(pool))
        shift = jnp.where(tok >= start, owner * most - start, shift)
        start = start + len_ref[0, r]
    out_ref[...] = tok + shift


def down_kernel(core_ref, code_ref, x_ref, d_ref, keep_ref, send_ref, *, pool):
    half, lanes = keep_ref.shape
    rank = lanes // 2
    every = lax.dot_general(x_ref[...], d_ref[...], (((1,), (1,)), ((), ())), preferred_element_type=F32)
    code = code_ref[...]
    acc = jnp.zeros(code.shape, F32)
    for b in range(pool // 2):
        acc = acc + jnp.where(code == 2 * b, every[:, 2 * b * rank:2 * (b + 1) * rank], 0.0)
    acc = acc + pltpu.roll(acc, rank, 1)
    first = lax.broadcasted_iota(jnp.int32, (half, lanes), 1) < rank
    top = jnp.where(first, acc[:half], acc[2 * half:3 * half]).astype(BF)
    low = jnp.where(first, acc[half:2 * half], acc[3 * half:]).astype(BF)
    core = core_ref[0]

    @pl.when(core == 0)
    def _():
        keep_ref[...] = top
        send_ref[...] = low

    @pl.when(core != 0)
    def _():
        keep_ref[...] = low
        send_ref[...] = top


def up_kernel(core_ref, code_ref, low_ref, u_ref, *rest, pool, flip):
    out_ref, o_buf, o_sem = rest[-3:]
    rows, lanes = low_ref.shape
    rank = lanes // 2
    which = core_ref[0] ^ flip
    packed = low_ref[...].astype(F32)
    turned = pltpu.roll(packed, rank, 1)
    first = lax.broadcasted_iota(jnp.int32, packed.shape, 1) < rank
    leaving = []
    for i in range(2):
        low = jnp.where(first, packed, turned) if i == 0 else jnp.where(first, turned, packed)
        at = pl.ds(pl.multiple_of((2 * i + which) * rows, rows), rows)
        code = code_ref[at, :]
        spread = jnp.concatenate(
            [jnp.where(code == 2 * k, low, 0.0).astype(BF) for k in range(pool // 2)], 1
        )
        o_buf[i] = jnp.dot(spread, u_ref[...], preferred_element_type=F32).astype(BF)
        leaving.append(pltpu.make_async_copy(o_buf.at[i], out_ref.at[at], o_sem.at[i]))
        leaving[-1].start()
    for copy in leaving:
        copy.wait()


def pair_dot_kernel(t_ref, x_ref, w_ref, out_ref):
    out_ref[0] = jnp.dot(x_ref[...], w_ref[...], preferred_element_type=F32).astype(BF)


def own_dot_kernel(t_ref, x_ref, w_ref, p_ref, a0_ref, b0_ref, a1_ref, b1_ref):
    half = x_ref.shape[0] // 2
    j = pl.program_id(0)
    came = p_ref[j if p_ref.shape[0] > 1 else 0].astype(F32)
    both = (jnp.dot(x_ref[...], w_ref[...], preferred_element_type=F32) + came).astype(BF)

    @pl.when(j == 0)
    def _():
        a0_ref[...] = both[:half]
        b0_ref[...] = both[half:]

    @pl.when(j == 1)
    def _():
        a1_ref[...] = both[:half]
        b1_ref[...] = both[half:]


def before_kernel(res_ref, ka_ref, ra_ref, za_ref, kb_ref, rb_ref, zb_ref, left_ref, right_ref):
    half = ka_ref.shape[0]
    wide = left_ref.shape[1]
    base_a = ka_ref[...].astype(F32) + ra_ref[...].astype(F32) + za_ref[...].astype(F32)
    base_b = kb_ref[...].astype(F32) + rb_ref[...].astype(F32) + zb_ref[...].astype(F32)
    top = res_ref[:half].astype(F32) + base_a
    low = res_ref[half:].astype(F32) + base_b
    left_ref[:half] = top[:, :wide]
    left_ref[half:] = low[:, :wide]
    right_ref[:half] = top[:, wide:]
    right_ref[half:] = low[:, wide:]


def final_kernel(row_ref, ret_ref, left_ref, right_ref, out_ref, sel_ref, p_buf, o_buf, p_sem, o_sem):
    n = out_ref.shape[1] // PARTS
    near_parts = left_ref.shape[1] // n
    at = [pl.ds(i * n, n) for i in range(PARTS)]
    coming = [
        pltpu.make_async_copy(right_ref.at[:, at[i]], p_buf.at[i], p_sem.at[i]) for i in range(PARTS - near_parts)
    ]
    leaving = [pltpu.make_async_copy(o_buf.at[i], out_ref.at[:, at[i]], o_sem.at[i]) for i in range(PARTS)]
    for copy in coming:
        copy.start()
    lanes = row_ref.shape[1]
    row = row_ref[...] - lax.broadcasted_iota(jnp.int32, row_ref.shape, 1)
    for k in range(sel_ref.shape[1] // lanes):
        sel_ref[:, k * lanes:(k + 1) * lanes] = jnp.where(row == k * lanes, 1.0, 0.0).astype(BF)
    for i in range(PARTS):
        delta = jnp.dot(sel_ref[...], ret_ref[:, at[i]], preferred_element_type=F32)
        if i < near_parts:
            pre = left_ref[:, at[i]]
        else:
            coming[i - near_parts].wait()
            pre = p_buf[i - near_parts]
        o_buf[i] = (pre + delta).astype(BF)
        leaving[i].start()
    for copy in leaving:
        copy.wait()


def fetch_kernel(x_ref, out_ref, sem):
    copy = pltpu.make_async_copy(x_ref, out_ref, sem)
    copy.start()
    copy.wait()


def sum_kernel(*refs):
    acc = refs[0][...].astype(F32)
    for r in refs[1:-1]:
        acc = acc + r[...].astype(F32)
    refs[-1][...] = acc.astype(BF)


def near(v):
    return pltpu.with_memory_space_constraint(v, pltpu.VMEM)


def far(v):
    return pltpu.with_memory_space_constraint(v, pltpu.HBM)


def one_block(x, residual, weight, down, up, pool_slot, req_id, req_len):
    groups = lax.axis_size("req")
    n_t = lax.axis_size("tensor")
    me = lax.axis_index("req").astype(jnp.int32)
    t = lax.axis_index("tensor").astype(jnp.int32)
    tokens, features = x.shape
    pool = down.shape[0]
    rank = down.shape[2]
    cols = residual.shape[1]
    requests = req_len.shape[1]
    most = 2 * tokens // requests
    slots = groups * most
    half = tokens // 2
    me1 = me.reshape(1)
    t1 = t.reshape(1)
    xor = lambda m: [(i, i ^ m) for i in range(n_t)]
    sds = jax.ShapeDtypeStruct

    outgoing = pl.pallas_call(
        functools.partial(pack_kernel, pool=pool, most=most),
        out_shape=sds((slots, features), BF),
        in_specs=[SM, SM, SM, SM, VM],
        out_specs=VM,
        scratch_shapes=[pltpu.VMEM((slots, tokens), BF)],
        cost_estimate=cost(2 * slots * tokens * features, 2 * (slots + tokens) * features),
        name="pack",
    )(me1, req_len, req_id, pool_slot, x)
    arrived = lax.all_to_all(outgoing.reshape(groups, most, features), "req", split_axis=0, concat_axis=0, tiled=True)

    def parts(offsets, x):
        def order(j):
            return jnp.where(j == 0, offsets[0], offsets[1])

        n = len(offsets)
        flops = 2 * tokens * features * cols * n
        whole = pl.BlockSpec((tokens, features), lambda j, t_ref: (0, 0))
        out = pl.pallas_call(
            pair_dot_kernel,
            out_shape=sds((n, tokens, cols), BF),
            grid_spec=pltpu.PrefetchScalarGridSpec(
                num_scalar_prefetch=1,
                grid=(n,),
                in_specs=[whole, pl.BlockSpec((features, cols), lambda j, t_ref: (0, t_ref[0] ^ 1 ^ (2 * order(j))))],
                out_specs=pl.BlockSpec((1, tokens, cols), lambda j, t_ref: (j, 0, 0)),
            ),
            cost_estimate=cost(flops, 2 * n * cols * (tokens + features)),
            name="pair_dot",
        )(t1, x, weight)

        def own(x, came, close):
            piece = sds((half, cols), BF)
            keep = pl.BlockSpec((half, cols), lambda j, t_ref: (0, 0))
            return pl.pallas_call(
                own_dot_kernel,
                out_shape=[piece] * 4,
                grid_spec=pltpu.PrefetchScalarGridSpec(
                    num_scalar_prefetch=1,
                    grid=(n,),
                    in_specs=[
                        whole,
                        pl.BlockSpec((features, cols), lambda j, t_ref: (0, t_ref[0] ^ (2 * order(j)))),
                        VM if close else pl.BlockSpec((1, tokens, cols), lambda j, t_ref: (j, 0, 0)),
                    ],
                    out_specs=[keep] * 4,
                ),
                cost_estimate=cost(flops, 2 * n * cols * (2 * tokens + features)),
                name="own_dot",
            )(t1, x, weight, near(came) if close else came)

        return out, own

    x, _ = lax.optimization_barrier((x, outgoing))
    to_1, own_1 = parts((2, 1), x)
    from_1 = lax.ppermute(to_1, "tensor", xor(1))
    x, _ = lax.optimization_barrier((x, to_1))
    to_2, own_2 = parts((3, 0), x)
    from_2 = lax.ppermute(to_2, "tensor", xor(1))
    x, _ = lax.optimization_barrier((x, to_2))
    s2a, s2b, s1a, k1b = own_1(x, from_1, True)
    r2a = lax.ppermute(s2a, "tensor", xor(2))
    r2b = lax.ppermute(s2b, "tensor", xor(6))
    x, req_id2, pool_slot2, up, _ = lax.optimization_barrier((x, req_id, pool_slot, up, s2a))

    ids = jnp.arange(pool_slot.shape[0], dtype=jnp.int32)
    held = me * pool + jnp.arange(pool, dtype=jnp.int32)
    id_of = jnp.sum(jnp.where(pool_slot2[None, :] == held[:, None], ids[None, :], 0), 1)
    uses = req_id2[:, :, None] == id_of[None, None, :]
    idx = jnp.sum(jnp.where(uses, jnp.arange(pool, dtype=jnp.int32), 0), (1, 2))
    lane = jnp.arange(2 * rank, dtype=jnp.int32)
    code = jnp.broadcast_to(idx[:, None, None], (groups, most, 2 * rank)) - jnp.where(lane < rank, 0, 1)
    code = code.reshape(slots, 2 * rank)

    up_maps = pl.pallas_call(
        fetch_kernel,
        out_shape=pltpu.VMEM((pool * rank, cols), BF),
        in_specs=[HB],
        out_specs=VM,
        scratch_shapes=[DMA],
        cost_estimate=cost(0, 4 * pool * rank * cols),
        name="fetch_up",
        compiler_params=SMALL,
    )(far(up.reshape(pool * rank, cols)))

    arrived, code, up_maps = lax.optimization_barrier((arrived, code, up_maps))
    code = near(code)
    core = t1 & 1
    piece = pltpu.VMEM((slots // 4, 2 * rank), BF)
    low, send = pl.pallas_call(
        functools.partial(down_kernel, pool=pool),
        out_shape=[piece] * 2,
        in_specs=[SM, VM, VM, VM],
        out_specs=[VM] * 2,
        cost_estimate=cost(2 * slots * pool * rank * features, 2 * slots * features),
        name="down",
        compiler_params=SMALL,
    )(
        core,
        code,
        near(arrived.reshape(slots, features)),
        near(jnp.swapaxes(down, 1, 2).reshape(pool * rank, features)),
    )

    def total(*terms):
        return pl.pallas_call(
            sum_kernel,
            out_shape=piece,
            in_specs=[VM] * len(terms),
            out_specs=VM,
            name="sum_low",
            compiler_params=SMALL,
        )(*[near(v) for v in terms])

    low = total(low, lax.ppermute(send, "tensor", xor(1)))
    came = []
    for m in (4, 2, 6):
        came.append(lax.ppermute(low, "tensor", xor(m)))
    low = total(low, *came)
    other = lax.ppermute(low, "tensor", xor(1))

    def lift(rows_low, flip, filled=()):
        return pl.pallas_call(
            functools.partial(up_kernel, pool=pool, flip=flip),
            out_shape=pltpu.HBM((slots, cols), BF),
            in_specs=[SM, VM, VM, VM] + [HB] * len(filled),
            out_specs=HB,
            scratch_shapes=[pltpu.VMEM((2, slots // 4, cols), BF), DMA((2,))],
            input_output_aliases={4: 0} if filled else {},
            cost_estimate=cost(slots * pool * rank * cols, slots * cols),
            name="up",
            compiler_params=SMALL,
        )(core, code, near(rows_low), near(up_maps), *filled)

    raised = lift(low, 0)
    raised = lift(other, 1, (raised,))
    raised, s1a, k1b, x, me1 = lax.optimization_barrier((raised, s1a, k1b, x, me1))
    returned = lax.all_to_all(
        raised.reshape(groups, most, cols), "req", split_axis=0, concat_axis=0, tiled=True
    )

    row = pl.pallas_call(
        functools.partial(unpack_index_kernel, pool=pool, most=most),
        out_shape=pltpu.VMEM((tokens, 128), jnp.int32),
        in_specs=[SM, SM, SM, SM],
        out_specs=VM,
        cost_estimate=cost(64 * 128 * tokens, 4 * 128 * tokens),
        name="unpack_index",
    compiler_params=SMALL,
    )(me1, req_len, req_id, pool_slot)

    k3a, s3b, k0a, k0b = own_2(x, from_2, False)
    za = lax.ppermute((k3a.astype(F32) + r2a.astype(F32)).astype(BF), "tensor", xor(6))
    zb = lax.ppermute((k1b.astype(F32) + r2b.astype(F32)).astype(BF), "tensor", xor(2))
    r1a = lax.ppermute(s1a, "tensor", xor(2))
    r3b = lax.ppermute(s3b, "tensor", xor(6))

    wide = cols // PARTS
    left, right = pl.pallas_call(
        before_kernel,
        out_shape=[pltpu.VMEM((tokens, 2 * wide), F32), pltpu.HBM((tokens, cols - 2 * wide), F32)],
        in_specs=[VM] * 7,
        out_specs=[VM, VM],
        cost_estimate=cost(4 * tokens * cols, 12 * tokens * cols),
        name="before",
    )(residual, *[far(v) for v in (k0a, r1a, za, k0b, r3b, zb)])
    returned, left, right, row = lax.optimization_barrier((returned, left, right, row))
    return pl.pallas_call(
        final_kernel,
        out_shape=sds((tokens, cols), BF),
        in_specs=[VM, VM, VM, HB],
        out_specs=HB,
        scratch_shapes=[
            pltpu.VMEM((tokens, slots), BF),
            pltpu.VMEM((PARTS - 2, tokens, wide), F32),
            pltpu.VMEM((PARTS, tokens, wide), BF),
            DMA((PARTS - 2,)),
            DMA((PARTS,)),
        ],
        cost_estimate=cost(2 * tokens * slots * cols, 2 * cols * (slots + 4 * tokens)),
        name="final",
        compiler_params=pltpu.CompilerParams(vmem_limit_bytes=56 * 2**20),
    )(near(row), near(returned.reshape(slots, cols)), near(left), right)


def solution(mesh):
    in_specs = (
        P("req", "tensor"),
        P("req", "tensor"),
        P("tensor", None),
        P("req", "tensor", None),
        P("req", None, "tensor"),
        P(),
        P(),
        P("req", None),
    )
    return jax.shard_map(one_block, mesh=mesh, in_specs=in_specs, out_specs=P("req", "tensor"), check_vma=False)
```

```python
import functools

import jax
import jax.numpy as jnp
from jax import lax
from jax.experimental import pallas as pl
from jax.experimental.pallas import tpu as pltpu
from jax.sharding import PartitionSpec as P


BF = jnp.bfloat16
F32 = jnp.float32
VM = pl.BlockSpec(memory_space=pltpu.VMEM)
SM = pl.BlockSpec(memory_space=pltpu.SMEM)
HB = pl.BlockSpec(memory_space=pl.ANY)
DMA = pltpu.SemaphoreType.DMA
PARTS = 4


SMALL = pltpu.CompilerParams(vmem_limit_bytes=24 * 2**20)


def cost(flops, nbytes):
    return pl.CostEstimate(flops=int(flops), transcendentals=0, bytes_accessed=int(nbytes))


def pack_kernel(me_ref, len_ref, id_ref, slot_ref, x_ref, out_ref, sel_ref, o_buf, o_sem, *, pool, most):
    requests = len_ref.shape[1]
    tokens = x_ref.shape[0]
    rows = lax.broadcasted_iota(jnp.int32, (most, tokens), 0)
    ahead = lax.broadcasted_iota(jnp.int32, (most, tokens), 1) - rows
    me = me_ref[0]
    start = jnp.int32(0)
    for r in range(requests):
        owner = lax.div(slot_ref[id_ref[me, r]], jnp.int32(pool))
        at = pl.multiple_of(owner * most, most)
        sel_ref[pl.ds(at, most), :] = jnp.where(ahead == start, 1.0, 0.0).astype(BF)
        start = start + len_ref[0, r]
    n = o_buf.shape[1]
    leaving = []
    for i in range(2):
        at = pl.ds(i * n, n)
        o_buf[i] = jnp.dot(sel_ref[at, :], x_ref[...], preferred_element_type=F32).astype(BF)
        leaving.append(pltpu.make_async_copy(o_buf.at[i], out_ref.at[at], o_sem.at[i]))
        leaving[-1].start()
    for copy in leaving:
        copy.wait()


def unpack_index_kernel(me_ref, len_ref, id_ref, slot_ref, out_ref, *, pool, most):
    tok = lax.broadcasted_iota(jnp.int32, out_ref.shape, 0)
    me = me_ref[0]
    start = jnp.int32(0)
    shift = jnp.zeros(out_ref.shape, jnp.int32)
    for r in range(len_ref.shape[1]):
        owner = lax.div(slot_ref[id_ref[me, r]], jnp.int32(pool))
        shift = jnp.where(tok >= start, owner * most - start, shift)
        start = start + len_ref[0, r]
    out_ref[...] = tok + shift


def down_kernel(core_ref, code_ref, x_ref, d_ref, out_ref, *, pool, flip):
    rows, lanes = out_ref.shape
    rank = lanes // 2
    which = core_ref[0] ^ flip
    at = [pl.ds(pl.multiple_of((2 * i + which) * rows, rows), rows) for i in range(2)]
    x = jnp.concatenate([x_ref[at[0], :], x_ref[at[1], :]], 0)
    code = jnp.concatenate([code_ref[at[0], :], code_ref[at[1], :]], 0)
    every = lax.dot_general(x, d_ref[...], (((1,), (1,)), ((), ())), preferred_element_type=F32)
    acc = jnp.zeros(code.shape, F32)
    for b in range(pool // 2):
        acc = acc + jnp.where(code == 2 * b, every[:, 2 * b * rank:2 * (b + 1) * rank], 0.0)
    acc = acc + pltpu.roll(acc, rank, 1)
    first = lax.broadcasted_iota(jnp.int32, (rows, lanes), 1) < rank
    out_ref[...] = jnp.where(first, acc[:rows], acc[rows:]).astype(BF)


def up_kernel(core_ref, code_ref, low_ref, u_ref, *rest, pool, flip):
    out_ref, o_buf, o_sem = rest[-3:]
    rows, lanes = low_ref.shape
    rank = lanes // 2
    which = core_ref[0] ^ flip
    packed = low_ref[...].astype(F32)
    turned = pltpu.roll(packed, rank, 1)
    first = lax.broadcasted_iota(jnp.int32, packed.shape, 1) < rank
    leaving = []
    for i in range(2):
        low = jnp.where(first, packed, turned) if i == 0 else jnp.where(first, turned, packed)
        at = pl.ds(pl.multiple_of((2 * i + which) * rows, rows), rows)
        code = code_ref[at, :]
        spread = jnp.concatenate(
            [jnp.where(code == 2 * k, low, 0.0).astype(BF) for k in range(pool // 2)], 1
        )
        o_buf[i] = jnp.dot(spread, u_ref[...], preferred_element_type=F32).astype(BF)
        leaving.append(pltpu.make_async_copy(o_buf.at[i], out_ref.at[at], o_sem.at[i]))
        leaving[-1].start()
    for copy in leaving:
        copy.wait()


def pair_dot_kernel(t_ref, x_ref, w_ref, out_ref):
    out_ref[0] = jnp.dot(x_ref[...], w_ref[...], preferred_element_type=F32).astype(BF)


def own_dot_kernel(t_ref, x_ref, w_ref, p_ref, a0_ref, b0_ref, a1_ref, b1_ref):
    half = x_ref.shape[0] // 2
    j = pl.program_id(0)
    came = p_ref[j if p_ref.shape[0] > 1 else 0].astype(F32)
    both = (jnp.dot(x_ref[...], w_ref[...], preferred_element_type=F32) + came).astype(BF)

    @pl.when(j == 0)
    def _():
        a0_ref[...] = both[:half]
        b0_ref[...] = both[half:]

    @pl.when(j == 1)
    def _():
        a1_ref[...] = both[:half]
        b1_ref[...] = both[half:]


def before_kernel(res_ref, ka_ref, ra_ref, za_ref, kb_ref, rb_ref, zb_ref, left_ref, right_ref):
    half = ka_ref.shape[0]
    wide = left_ref.shape[1]
    base_a = ka_ref[...].astype(F32) + ra_ref[...].astype(F32) + za_ref[...].astype(F32)
    base_b = kb_ref[...].astype(F32) + rb_ref[...].astype(F32) + zb_ref[...].astype(F32)
    top = res_ref[:half].astype(F32) + base_a
    low = res_ref[half:].astype(F32) + base_b
    left_ref[:half] = top[:, :wide]
    left_ref[half:] = low[:, :wide]
    right_ref[:half] = top[:, wide:]
    right_ref[half:] = low[:, wide:]


def final_kernel(row_ref, ret_ref, left_ref, right_ref, out_ref, sel_ref, p_buf, o_buf, p_sem, o_sem):
    n = out_ref.shape[1] // PARTS
    near_parts = left_ref.shape[1] // n
    at = [pl.ds(i * n, n) for i in range(PARTS)]
    coming = [
        pltpu.make_async_copy(right_ref.at[:, at[i]], p_buf.at[i], p_sem.at[i]) for i in range(PARTS - near_parts)
    ]
    leaving = [pltpu.make_async_copy(o_buf.at[i], out_ref.at[:, at[i]], o_sem.at[i]) for i in range(PARTS)]
    for copy in coming:
        copy.start()
    lanes = row_ref.shape[1]
    row = row_ref[...] - lax.broadcasted_iota(jnp.int32, row_ref.shape, 1)
    for k in range(sel_ref.shape[1] // lanes):
        sel_ref[:, k * lanes:(k + 1) * lanes] = jnp.where(row == k * lanes, 1.0, 0.0).astype(BF)
    for i in range(PARTS):
        delta = jnp.dot(sel_ref[...], ret_ref[:, at[i]], preferred_element_type=F32)
        if i < near_parts:
            pre = left_ref[:, at[i]]
        else:
            coming[i - near_parts].wait()
            pre = p_buf[i - near_parts]
        o_buf[i] = (pre + delta).astype(BF)
        leaving[i].start()
    for copy in leaving:
        copy.wait()


def fetch_kernel(x_ref, out_ref, sem):
    copy = pltpu.make_async_copy(x_ref, out_ref, sem)
    copy.start()
    copy.wait()


def sum_kernel(*refs):
    acc = refs[0][...].astype(F32)
    for r in refs[1:-1]:
        acc = acc + r[...].astype(F32)
    refs[-1][...] = acc.astype(BF)


def near(v):
    return pltpu.with_memory_space_constraint(v, pltpu.VMEM)


def far(v):
    return pltpu.with_memory_space_constraint(v, pltpu.HBM)


def one_block(x, residual, weight, down, up, pool_slot, req_id, req_len):
    groups = lax.axis_size("req")
    n_t = lax.axis_size("tensor")
    me = lax.axis_index("req").astype(jnp.int32)
    t = lax.axis_index("tensor").astype(jnp.int32)
    tokens, features = x.shape
    pool = down.shape[0]
    rank = down.shape[2]
    cols = residual.shape[1]
    requests = req_len.shape[1]
    most = 2 * tokens // requests
    slots = groups * most
    half = tokens // 2
    me1 = me.reshape(1)
    t1 = t.reshape(1)
    xor = lambda m: [(i, i ^ m) for i in range(n_t)]
    sds = jax.ShapeDtypeStruct

    outgoing = pl.pallas_call(
        functools.partial(pack_kernel, pool=pool, most=most),
        out_shape=sds((slots, features), BF),
        in_specs=[SM, SM, SM, SM, VM],
        out_specs=HB,
        scratch_shapes=[pltpu.VMEM((slots, tokens), BF), pltpu.VMEM((2, slots // 2, features), BF), DMA((2,))],
        cost_estimate=cost(2 * slots * tokens * features, 2 * (slots + tokens) * features),
        name="pack",
    )(me1, req_len, req_id, pool_slot, x)
    arrived = lax.all_to_all(outgoing.reshape(groups, most, features), "req", split_axis=0, concat_axis=0, tiled=True)

    def parts(offsets, x):
        def order(j):
            return jnp.where(j == 0, offsets[0], offsets[1])

        n = len(offsets)
        flops = 2 * tokens * features * cols * n
        whole = pl.BlockSpec((tokens, features), lambda j, t_ref: (0, 0))
        out = pl.pallas_call(
            pair_dot_kernel,
            out_shape=sds((n, tokens, cols), BF),
            grid_spec=pltpu.PrefetchScalarGridSpec(
                num_scalar_prefetch=1,
                grid=(n,),
                in_specs=[whole, pl.BlockSpec((features, cols), lambda j, t_ref: (0, t_ref[0] ^ 1 ^ (2 * order(j))))],
                out_specs=pl.BlockSpec((1, tokens, cols), lambda j, t_ref: (j, 0, 0)),
            ),
            cost_estimate=cost(flops, 2 * n * cols * (tokens + features)),
            name="pair_dot",
        )(t1, x, weight)

        def own(x, came, close):
            piece = sds((half, cols), BF)
            keep = pl.BlockSpec((half, cols), lambda j, t_ref: (0, 0))
            return pl.pallas_call(
                own_dot_kernel,
                out_shape=[piece] * 4,
                grid_spec=pltpu.PrefetchScalarGridSpec(
                    num_scalar_prefetch=1,
                    grid=(n,),
                    in_specs=[
                        whole,
                        pl.BlockSpec((features, cols), lambda j, t_ref: (0, t_ref[0] ^ (2 * order(j)))),
                        VM if close else pl.BlockSpec((1, tokens, cols), lambda j, t_ref: (j, 0, 0)),
                    ],
                    out_specs=[keep] * 4,
                ),
                cost_estimate=cost(flops, 2 * n * cols * (2 * tokens + features)),
                name="own_dot",
            )(t1, x, weight, near(came) if close else came)

        return out, own

    x, _ = lax.optimization_barrier((x, outgoing))
    to_1, own_1 = parts((2, 1), x)
    from_1 = lax.ppermute(to_1, "tensor", xor(1))
    x, _ = lax.optimization_barrier((x, to_1))
    to_2, own_2 = parts((3, 0), x)
    from_2 = lax.ppermute(to_2, "tensor", xor(1))
    x, _ = lax.optimization_barrier((x, to_2))
    s2a, s2b, s1a, k1b = own_1(x, from_1, True)
    r2a = lax.ppermute(s2a, "tensor", xor(2))
    r2b = lax.ppermute(s2b, "tensor", xor(6))
    x, req_id2, pool_slot2, up, _ = lax.optimization_barrier((x, req_id, pool_slot, up, s2a))

    ids = jnp.arange(pool_slot.shape[0], dtype=jnp.int32)
    held = me * pool + jnp.arange(pool, dtype=jnp.int32)
    id_of = jnp.sum(jnp.where(pool_slot2[None, :] == held[:, None], ids[None, :], 0), 1)
    uses = req_id2[:, :, None] == id_of[None, None, :]
    idx = jnp.sum(jnp.where(uses, jnp.arange(pool, dtype=jnp.int32), 0), (1, 2))
    lane = jnp.arange(2 * rank, dtype=jnp.int32)
    code = jnp.broadcast_to(idx[:, None, None], (groups, most, 2 * rank)) - jnp.where(lane < rank, 0, 1)
    code = code.reshape(slots, 2 * rank)

    up_maps = pl.pallas_call(
        fetch_kernel,
        out_shape=pltpu.VMEM((pool * rank, cols), BF),
        in_specs=[HB],
        out_specs=VM,
        scratch_shapes=[DMA],
        cost_estimate=cost(0, 4 * pool * rank * cols),
        name="fetch_up",
        compiler_params=SMALL,
    )(far(up.reshape(pool * rank, cols)))

    arrived, code, up_maps = lax.optimization_barrier((arrived, code, up_maps))
    code = near(code)
    core = t1 & 1
    piece = pltpu.VMEM((slots // 4, 2 * rank), BF)
    rows_here = arrived.reshape(slots, features)
    down_maps = jnp.swapaxes(down, 1, 2).reshape(pool * rank, features)

    def lower(flip):
        return pl.pallas_call(
            functools.partial(down_kernel, pool=pool, flip=flip),
            out_shape=piece,
            in_specs=[SM, VM, VM, VM],
            out_specs=VM,
            cost_estimate=cost(slots * pool * rank * features, slots * features),
            name="down",
            compiler_params=SMALL,
        )(core, code, near(rows_here), near(down_maps))

    send = lower(1)
    other = lax.ppermute(send, "tensor", xor(1))
    rows_here, _ = lax.optimization_barrier((rows_here, send))
    low = lower(0)

    def total(*terms):
        return pl.pallas_call(
            sum_kernel,
            out_shape=piece,
            in_specs=[VM] * len(terms),
            out_specs=VM,
            name="sum_low",
            compiler_params=SMALL,
        )(*[near(v) for v in terms])

    low = total(low, other)
    came = []
    for m in (4, 2, 6):
        came.append(lax.ppermute(low, "tensor", xor(m)))
    low = total(low, *came)
    other = lax.ppermute(low, "tensor", xor(1))

    def lift(rows_low, flip, filled=()):
        return pl.pallas_call(
            functools.partial(up_kernel, pool=pool, flip=flip),
            out_shape=pltpu.HBM((slots, cols), BF),
            in_specs=[SM, VM, VM, VM] + [HB] * len(filled),
            out_specs=HB,
            scratch_shapes=[pltpu.VMEM((2, slots // 4, cols), BF), DMA((2,))],
            input_output_aliases={4: 0} if filled else {},
            cost_estimate=cost(slots * pool * rank * cols, slots * cols),
            name="up",
            compiler_params=SMALL,
        )(core, code, near(rows_low), near(up_maps), *filled)

    raised = lift(low, 0)
    raised = lift(other, 1, (raised,))
    raised, s1a, k1b, x, me1 = lax.optimization_barrier((raised, s1a, k1b, x, me1))
    returned = lax.all_to_all(
        raised.reshape(groups, most, cols), "req", split_axis=0, concat_axis=0, tiled=True
    )

    row = pl.pallas_call(
        functools.partial(unpack_index_kernel, pool=pool, most=most),
        out_shape=pltpu.VMEM((tokens, 128), jnp.int32),
        in_specs=[SM, SM, SM, SM],
        out_specs=VM,
        cost_estimate=cost(64 * 128 * tokens, 4 * 128 * tokens),
        name="unpack_index",
    compiler_params=SMALL,
    )(me1, req_len, req_id, pool_slot)

    k3a, s3b, k0a, k0b = own_2(x, from_2, False)
    za = lax.ppermute((k3a.astype(F32) + r2a.astype(F32)).astype(BF), "tensor", xor(6))
    zb = lax.ppermute((k1b.astype(F32) + r2b.astype(F32)).astype(BF), "tensor", xor(2))
    r1a = lax.ppermute(s1a, "tensor", xor(2))
    r3b = lax.ppermute(s3b, "tensor", xor(6))

    wide = cols // PARTS
    left, right = pl.pallas_call(
        before_kernel,
        out_shape=[pltpu.VMEM((tokens, 2 * wide), F32), pltpu.HBM((tokens, cols - 2 * wide), F32)],
        in_specs=[VM] * 7,
        out_specs=[VM, VM],
        cost_estimate=cost(4 * tokens * cols, 12 * tokens * cols),
        name="before",
    )(residual, *[far(v) for v in (k0a, r1a, za, k0b, r3b, zb)])
    returned, left, right, row = lax.optimization_barrier((returned, left, right, row))
    return pl.pallas_call(
        final_kernel,
        out_shape=sds((tokens, cols), BF),
        in_specs=[VM, VM, VM, HB],
        out_specs=HB,
        scratch_shapes=[
            pltpu.VMEM((tokens, slots), BF),
            pltpu.VMEM((PARTS - 2, tokens, wide), F32),
            pltpu.VMEM((PARTS, tokens, wide), BF),
            DMA((PARTS - 2,)),
            DMA((PARTS,)),
        ],
        cost_estimate=cost(2 * tokens * slots * cols, 2 * cols * (slots + 4 * tokens)),
        name="final",
        compiler_params=pltpu.CompilerParams(vmem_limit_bytes=56 * 2**20),
    )(near(row), near(returned.reshape(slots, cols)), near(left), right)


def solution(mesh):
    in_specs = (
        P("req", "tensor"),
        P("req", "tensor"),
        P("tensor", None),
        P("req", "tensor", None),
        P("req", None, "tensor"),
        P(),
        P(),
        P("req", None),
    )
    return jax.shard_map(one_block, mesh=mesh, in_specs=in_specs, out_specs=P("req", "tensor"), check_vma=False)
```

```python
import functools

import jax
import jax.numpy as jnp
from jax import lax
from jax.experimental import pallas as pl
from jax.experimental.pallas import tpu as pltpu
from jax.sharding import PartitionSpec as P


BF = jnp.bfloat16
F32 = jnp.float32
VM = pl.BlockSpec(memory_space=pltpu.VMEM)
SM = pl.BlockSpec(memory_space=pltpu.SMEM)
HB = pl.BlockSpec(memory_space=pl.ANY)
DMA = pltpu.SemaphoreType.DMA
PARTS = 4


SMALL = pltpu.CompilerParams(vmem_limit_bytes=24 * 2**20)


def cost(flops, nbytes):
    return pl.CostEstimate(flops=int(flops), transcendentals=0, bytes_accessed=int(nbytes))


def pack_kernel(me_ref, len_ref, id_ref, slot_ref, x_ref, out_ref, sel_ref, o_buf, o_sem, *, pool, most):
    requests = len_ref.shape[1]
    tokens = x_ref.shape[0]
    rows = lax.broadcasted_iota(jnp.int32, (most, tokens), 0)
    ahead = lax.broadcasted_iota(jnp.int32, (most, tokens), 1) - rows
    me = me_ref[0]
    start = jnp.int32(0)
    for r in range(requests):
        owner = lax.div(slot_ref[id_ref[me, r]], jnp.int32(pool))
        at = pl.multiple_of(owner * most, most)
        sel_ref[pl.ds(at, most), :] = jnp.where(ahead == start, 1.0, 0.0).astype(BF)
        start = start + len_ref[0, r]
    n = o_buf.shape[1]
    leaving = []
    for i in range(2):
        at = pl.ds(i * n, n)
        o_buf[i] = jnp.dot(sel_ref[at, :], x_ref[...], preferred_element_type=F32).astype(BF)
        leaving.append(pltpu.make_async_copy(o_buf.at[i], out_ref.at[at], o_sem.at[i]))
        leaving[-1].start()
    for copy in leaving:
        copy.wait()


def unpack_index_kernel(me_ref, len_ref, id_ref, slot_ref, out_ref, *, pool, most):
    tok = lax.broadcasted_iota(jnp.int32, out_ref.shape, 0)
    me = me_ref[0]
    start = jnp.int32(0)
    shift = jnp.zeros(out_ref.shape, jnp.int32)
    for r in range(len_ref.shape[1]):
        owner = lax.div(slot_ref[id_ref[me, r]], jnp.int32(pool))
        shift = jnp.where(tok >= start, owner * most - start, shift)
        start = start + len_ref[0, r]
    out_ref[...] = tok + shift


def down_kernel(core_ref, code_ref, x_ref, d_ref, out_ref, *, pool, flip):
    rows, lanes = out_ref.shape
    rank = lanes // 2
    which = core_ref[0] ^ flip
    at = [pl.ds(pl.multiple_of((2 * i + which) * rows, rows), rows) for i in range(2)]
    x = jnp.concatenate([x_ref[at[0], :], x_ref[at[1], :]], 0)
    code = jnp.concatenate([code_ref[at[0], :], code_ref[at[1], :]], 0)
    every = lax.dot_general(x, d_ref[...], (((1,), (1,)), ((), ())), preferred_element_type=F32)
    acc = jnp.zeros(code.shape, F32)
    for b in range(pool // 2):
        acc = acc + jnp.where(code == 2 * b, every[:, 2 * b * rank:2 * (b + 1) * rank], 0.0)
    acc = acc + pltpu.roll(acc, rank, 1)
    first = lax.broadcasted_iota(jnp.int32, (rows, lanes), 1) < rank
    out_ref[...] = jnp.where(first, acc[:rows], acc[rows:]).astype(BF)


def up_kernel(core_ref, code_ref, low_ref, u_ref, *rest, pool, flip):
    out_ref, o_buf, o_sem = rest[-3:]
    rows, lanes = low_ref.shape
    rank = lanes // 2
    which = core_ref[0] ^ flip
    packed = low_ref[...].astype(F32)
    turned = pltpu.roll(packed, rank, 1)
    first = lax.broadcasted_iota(jnp.int32, packed.shape, 1) < rank
    leaving = []
    for i in range(2):
        low = jnp.where(first, packed, turned) if i == 0 else jnp.where(first, turned, packed)
        at = pl.ds(pl.multiple_of((2 * i + which) * rows, rows), rows)
        code = code_ref[at, :]
        spread = jnp.concatenate(
            [jnp.where(code == 2 * k, low, 0.0).astype(BF) for k in range(pool // 2)], 1
        )
        n = rows // 2
        for h in range(2):
            o_buf[2 * i + h] = jnp.dot(
                spread[h * n:(h + 1) * n], u_ref[...], preferred_element_type=F32
            ).astype(BF)
            to = pl.ds(pl.multiple_of((2 * i + which) * rows + h * n, n), n)
            leaving.append(pltpu.make_async_copy(o_buf.at[2 * i + h], out_ref.at[to], o_sem.at[2 * i + h]))
            leaving[-1].start()
    for copy in leaving:
        copy.wait()


def pair_dot_kernel(t_ref, x_ref, w_ref, out_ref):
    out_ref[0] = jnp.dot(x_ref[...], w_ref[...], preferred_element_type=F32).astype(BF)


def own_dot_kernel(t_ref, x_ref, w_ref, p_ref, a0_ref, b0_ref, a1_ref, b1_ref):
    half = x_ref.shape[0] // 2
    j = pl.program_id(0)
    came = p_ref[j if p_ref.shape[0] > 1 else 0].astype(F32)
    both = (jnp.dot(x_ref[...], w_ref[...], preferred_element_type=F32) + came).astype(BF)

    @pl.when(j == 0)
    def _():
        a0_ref[...] = both[:half]
        b0_ref[...] = both[half:]

    @pl.when(j == 1)
    def _():
        a1_ref[...] = both[:half]
        b1_ref[...] = both[half:]


def before_kernel(res_ref, ka_ref, ra_ref, za_ref, kb_ref, rb_ref, zb_ref, left_ref, right_ref):
    half = ka_ref.shape[0]
    wide = left_ref.shape[1]
    base_a = ka_ref[...].astype(F32) + ra_ref[...].astype(F32) + za_ref[...].astype(F32)
    base_b = kb_ref[...].astype(F32) + rb_ref[...].astype(F32) + zb_ref[...].astype(F32)
    top = res_ref[:half].astype(F32) + base_a
    low = res_ref[half:].astype(F32) + base_b
    left_ref[:half] = top[:, :wide]
    left_ref[half:] = low[:, :wide]
    right_ref[:half] = top[:, wide:]
    right_ref[half:] = low[:, wide:]


def final_kernel(row_ref, ret_ref, left_ref, right_ref, out_ref, sel_ref, p_buf, o_buf, p_sem, o_sem):
    n = out_ref.shape[1] // PARTS
    near_parts = left_ref.shape[1] // n
    at = [pl.ds(i * n, n) for i in range(PARTS)]
    coming = [
        pltpu.make_async_copy(right_ref.at[:, at[i]], p_buf.at[i], p_sem.at[i]) for i in range(PARTS - near_parts)
    ]
    leaving = [pltpu.make_async_copy(o_buf.at[i], out_ref.at[:, at[i]], o_sem.at[i]) for i in range(PARTS)]
    for copy in coming:
        copy.start()
    lanes = row_ref.shape[1]
    row = row_ref[...] - lax.broadcasted_iota(jnp.int32, row_ref.shape, 1)
    for k in range(sel_ref.shape[1] // lanes):
        sel_ref[:, k * lanes:(k + 1) * lanes] = jnp.where(row == k * lanes, 1.0, 0.0).astype(BF)
    for i in range(PARTS):
        delta = jnp.dot(sel_ref[...], ret_ref[:, at[i]], preferred_element_type=F32)
        if i < near_parts:
            pre = left_ref[:, at[i]]
        else:
            coming[i - near_parts].wait()
            pre = p_buf[i - near_parts]
        o_buf[i] = (pre + delta).astype(BF)
        leaving[i].start()
    for copy in leaving:
        copy.wait()


def fetch_kernel(x_ref, out_ref, sem):
    copy = pltpu.make_async_copy(x_ref, out_ref, sem)
    copy.start()
    copy.wait()


def sum_kernel(*refs):
    acc = refs[0][...].astype(F32)
    for r in refs[1:-1]:
        acc = acc + r[...].astype(F32)
    refs[-1][...] = acc.astype(BF)


def near(v):
    return pltpu.with_memory_space_constraint(v, pltpu.VMEM)


def far(v):
    return pltpu.with_memory_space_constraint(v, pltpu.HBM)


def one_block(x, residual, weight, down, up, pool_slot, req_id, req_len):
    groups = lax.axis_size("req")
    n_t = lax.axis_size("tensor")
    me = lax.axis_index("req").astype(jnp.int32)
    t = lax.axis_index("tensor").astype(jnp.int32)
    tokens, features = x.shape
    pool = down.shape[0]
    rank = down.shape[2]
    cols = residual.shape[1]
    requests = req_len.shape[1]
    most = 2 * tokens // requests
    slots = groups * most
    half = tokens // 2
    me1 = me.reshape(1)
    t1 = t.reshape(1)
    xor = lambda m: [(i, i ^ m) for i in range(n_t)]
    sds = jax.ShapeDtypeStruct

    outgoing = pl.pallas_call(
        functools.partial(pack_kernel, pool=pool, most=most),
        out_shape=sds((slots, features), BF),
        in_specs=[SM, SM, SM, SM, VM],
        out_specs=HB,
        scratch_shapes=[pltpu.VMEM((slots, tokens), BF), pltpu.VMEM((2, slots // 2, features), BF), DMA((2,))],
        cost_estimate=cost(2 * slots * tokens * features, 2 * (slots + tokens) * features),
        name="pack",
    )(me1, req_len, req_id, pool_slot, x)
    arrived = lax.all_to_all(outgoing.reshape(groups, most, features), "req", split_axis=0, concat_axis=0, tiled=True)

    def parts(offsets, x):
        def order(j):
            return jnp.where(j == 0, offsets[0], offsets[1])

        n = len(offsets)
        flops = 2 * tokens * features * cols * n
        whole = pl.BlockSpec((tokens, features), lambda j, t_ref: (0, 0))
        out = pl.pallas_call(
            pair_dot_kernel,
            out_shape=sds((n, tokens, cols), BF),
            grid_spec=pltpu.PrefetchScalarGridSpec(
                num_scalar_prefetch=1,
                grid=(n,),
                in_specs=[whole, pl.BlockSpec((features, cols), lambda j, t_ref: (0, t_ref[0] ^ 1 ^ (2 * order(j))))],
                out_specs=pl.BlockSpec((1, tokens, cols), lambda j, t_ref: (j, 0, 0)),
            ),
            cost_estimate=cost(flops, 2 * n * cols * (tokens + features)),
            name="pair_dot",
        )(t1, x, weight)

        def own(x, came, close):
            piece = sds((half, cols), BF)
            keep = pl.BlockSpec((half, cols), lambda j, t_ref: (0, 0))
            return pl.pallas_call(
                own_dot_kernel,
                out_shape=[piece] * 4,
                grid_spec=pltpu.PrefetchScalarGridSpec(
                    num_scalar_prefetch=1,
                    grid=(n,),
                    in_specs=[
                        whole,
                        pl.BlockSpec((features, cols), lambda j, t_ref: (0, t_ref[0] ^ (2 * order(j)))),
                        VM if close else pl.BlockSpec((1, tokens, cols), lambda j, t_ref: (j, 0, 0)),
                    ],
                    out_specs=[keep] * 4,
                ),
                cost_estimate=cost(flops, 2 * n * cols * (2 * tokens + features)),
                name="own_dot",
            )(t1, x, weight, near(came) if close else came)

        return out, own

    x, _ = lax.optimization_barrier((x, outgoing))
    to_1, own_1 = parts((2, 1), x)
    from_1 = lax.ppermute(to_1, "tensor", xor(1))
    x, _ = lax.optimization_barrier((x, to_1))
    to_2, own_2 = parts((3, 0), x)
    from_2 = lax.ppermute(to_2, "tensor", xor(1))
    x, _ = lax.optimization_barrier((x, to_2))
    s2a, s2b, s1a, k1b = own_1(x, from_1, True)
    r2a = lax.ppermute(s2a, "tensor", xor(2))
    r2b = lax.ppermute(s2b, "tensor", xor(6))
    x, req_id2, pool_slot2, up, _ = lax.optimization_barrier((x, req_id, pool_slot, up, s2a))

    ids = jnp.arange(pool_slot.shape[0], dtype=jnp.int32)
    held = me * pool + jnp.arange(pool, dtype=jnp.int32)
    id_of = jnp.sum(jnp.where(pool_slot2[None, :] == held[:, None], ids[None, :], 0), 1)
    uses = req_id2[:, :, None] == id_of[None, None, :]
    idx = jnp.sum(jnp.where(uses, jnp.arange(pool, dtype=jnp.int32), 0), (1, 2))
    lane = jnp.arange(2 * rank, dtype=jnp.int32)
    code = jnp.broadcast_to(idx[:, None, None], (groups, most, 2 * rank)) - jnp.where(lane < rank, 0, 1)
    code = code.reshape(slots, 2 * rank)

    up_maps = pl.pallas_call(
        fetch_kernel,
        out_shape=pltpu.VMEM((pool * rank, cols), BF),
        in_specs=[HB],
        out_specs=VM,
        scratch_shapes=[DMA],
        cost_estimate=cost(0, 4 * pool * rank * cols),
        name="fetch_up",
        compiler_params=SMALL,
    )(far(up.reshape(pool * rank, cols)))

    arrived, code, up_maps = lax.optimization_barrier((arrived, code, up_maps))
    code = near(code)
    core = t1 & 1
    piece = pltpu.VMEM((slots // 4, 2 * rank), BF)
    rows_here = arrived.reshape(slots, features)
    down_maps = jnp.swapaxes(down, 1, 2).reshape(pool * rank, features)

    def lower(flip):
        return pl.pallas_call(
            functools.partial(down_kernel, pool=pool, flip=flip),
            out_shape=piece,
            in_specs=[SM, VM, VM, VM],
            out_specs=VM,
            cost_estimate=cost(slots * pool * rank * features, slots * features),
            name="down",
            compiler_params=SMALL,
        )(core, code, near(rows_here), near(down_maps))

    send = lower(1)
    other = lax.ppermute(send, "tensor", xor(1))
    rows_here, _ = lax.optimization_barrier((rows_here, send))
    low = lower(0)

    def total(*terms):
        return pl.pallas_call(
            sum_kernel,
            out_shape=piece,
            in_specs=[VM] * len(terms),
            out_specs=VM,
            name="sum_low",
            compiler_params=SMALL,
        )(*[near(v) for v in terms])

    low = total(low, other)
    came = []
    for m in (4, 2, 6):
        came.append(lax.ppermute(low, "tensor", xor(m)))
    low = total(low, *came)
    other = lax.ppermute(low, "tensor", xor(1))

    def lift(rows_low, flip, filled=()):
        return pl.pallas_call(
            functools.partial(up_kernel, pool=pool, flip=flip),
            out_shape=pltpu.HBM((slots, cols), BF),
            in_specs=[SM, VM, VM, VM] + [HB] * len(filled),
            out_specs=HB,
            scratch_shapes=[pltpu.VMEM((4, slots // 8, cols), BF), DMA((4,))],
            input_output_aliases={4: 0} if filled else {},
            cost_estimate=cost(slots * pool * rank * cols, slots * cols),
            name="up",
            compiler_params=SMALL,
        )(core, code, near(rows_low), near(up_maps), *filled)

    raised = lift(low, 0)
    raised = lift(other, 1, (raised,))
    raised, s1a, k1b, x, me1 = lax.optimization_barrier((raised, s1a, k1b, x, me1))
    returned = lax.all_to_all(
        raised.reshape(groups, most, cols), "req", split_axis=0, concat_axis=0, tiled=True
    )

    row = pl.pallas_call(
        functools.partial(unpack_index_kernel, pool=pool, most=most),
        out_shape=pltpu.VMEM((tokens, 128), jnp.int32),
        in_specs=[SM, SM, SM, SM],
        out_specs=VM,
        cost_estimate=cost(64 * 128 * tokens, 4 * 128 * tokens),
        name="unpack_index",
    compiler_params=SMALL,
    )(me1, req_len, req_id, pool_slot)

    k3a, s3b, k0a, k0b = own_2(x, from_2, False)
    za = lax.ppermute((k3a.astype(F32) + r2a.astype(F32)).astype(BF), "tensor", xor(6))
    zb = lax.ppermute((k1b.astype(F32) + r2b.astype(F32)).astype(BF), "tensor", xor(2))
    r1a = lax.ppermute(s1a, "tensor", xor(2))
    r3b = lax.ppermute(s3b, "tensor", xor(6))

    wide = cols // PARTS
    left, right = pl.pallas_call(
        before_kernel,
        out_shape=[pltpu.VMEM((tokens, 2 * wide), F32), pltpu.HBM((tokens, cols - 2 * wide), F32)],
        in_specs=[VM] * 7,
        out_specs=[VM, VM],
        cost_estimate=cost(4 * tokens * cols, 12 * tokens * cols),
        name="before",
    )(residual, *[far(v) for v in (k0a, r1a, za, k0b, r3b, zb)])
    returned, left, right, row = lax.optimization_barrier((returned, left, right, row))
    return pl.pallas_call(
        final_kernel,
        out_shape=sds((tokens, cols), BF),
        in_specs=[VM, VM, VM, HB],
        out_specs=HB,
        scratch_shapes=[
            pltpu.VMEM((tokens, slots), BF),
            pltpu.VMEM((PARTS - 2, tokens, wide), F32),
            pltpu.VMEM((PARTS, tokens, wide), BF),
            DMA((PARTS - 2,)),
            DMA((PARTS,)),
        ],
        cost_estimate=cost(2 * tokens * slots * cols, 2 * cols * (slots + 4 * tokens)),
        name="final",
        compiler_params=pltpu.CompilerParams(vmem_limit_bytes=56 * 2**20),
    )(near(row), near(returned.reshape(slots, cols)), near(left), right)


def solution(mesh):
    in_specs = (
        P("req", "tensor"),
        P("req", "tensor"),
        P("tensor", None),
        P("req", "tensor", None),
        P("req", None, "tensor"),
        P(),
        P(),
        P("req", None),
    )
    return jax.shard_map(one_block, mesh=mesh, in_specs=in_specs, out_specs=P("req", "tensor"), check_vma=False)
```
